128 devices in a mesh: xy: 8 (over y, core), gz: 16 (over z, x).
Axes of the slice: x: 4, y: 4, z: 4, core: 2. Of those that a mesh axis runs over, the one named last changes fastest.
Arguments:
- concentration: float32 [256, 64, 4096], P('gz', None, 'xy'), may hold values from -1 to 1
- geometry: float32 [2, 4096], P(None, 'xy'), may hold values from 0.5 to 2
- nbr_elem: int32 [4, 4096], P(None, 'xy'), may hold values from -1 to 4095, as said below
- nbr_edge: int32 [4, 4096], P(None, 'xy'), may hold values from 0 to 7, as said below
- wall_flags: int32 [256], P('gz'), may hold values 0 or 1
Outputs:
- modes: float32 [256, 64, 4096], P('gz', None, 'xy')
The draws below stay inside these ranges and needn't reach their ends.
Inputs may be any that keep to these rules, and one draw needn't show every extreme that they name: `nbr_elem`: entry [a, e] is the global number of the element across local edge a of element e, or -1 where that edge lies on a wall of the slab; the pairing is mutual. The neighbour is held by the same index of xy or by the index just before or after it, wrapping around; an element with a neighbour on the index before is among the first 64 elements of its device, one with a neighbour on the index after is among the last 64. No element has more than one edge whose neighbour is held by another index of xy. `nbr_edge`: the neighbour's local edge, plus 4 where the two elements number the shared nodes in opposite orders; 0 at walls; the same pairing read from both sides.
All inputs are finite; a program needn't handle non-finite values. No bound on the sum of `wall_flags` on one device may be relied on, other than what follows from the above.
Results may differ from the reference program's by a relative error of at most 0.0001.
Values sent between devices are 32-bit elements; how exact they have to be, the bound alone decides.
A program may use at most 128 MiB of HBM per device.

```python
import math
import jax
import jax.numpy as jnp
import numpy as np
from jax import lax

NZ = 256
NODES = 64
COLS = 8
ROWS = 64
ITERS = 2
ELEMS = 4096


def connect_tables(key):
    cells = ELEMS
    columns = cells // ROWS
    cell_ids = jnp.arange(cells, dtype=jnp.int32)
    column = cell_ids // ROWS
    height = cell_ids % ROWS
    device = column // COLS
    within = column % COLS
    band_id = jnp.where(within == 0, 0, jnp.where(within == COLS - 1, 2, 1))
    shuffle = jax.random.permutation(jax.random.fold_in(key, 101), cells).astype(jnp.int32)
    ranking = (device * 3 + band_id) * cells + shuffle
    sorted_ids = jnp.argsort(ranking)
    number = jnp.zeros(cells, jnp.int32).at[sorted_ids].set(cell_ids)
    flip_bits = jax.random.randint(jax.random.fold_in(key, 202), (2, cells), 0, 2).astype(jnp.int32)
    flip_x = flip_bits[0]
    flip_y = flip_bits[1]
    elem_tab = jnp.zeros((4, cells), jnp.int32)
    edge_tab = jnp.zeros((4, cells), jnp.int32)
    offsets = ((0, -1), (1, 0), (0, 1), (-1, 0))
    for global_side in range(4):
        step_x, step_y = offsets[global_side]
        next_col = (column + step_x) % columns
        next_row = height + step_y
        inside = (next_row >= 0) & (next_row < ROWS)
        next_cell = next_col * ROWS + jnp.clip(next_row, 0, ROWS - 1)
        if global_side % 2 == 0:
            label_me = flip_y
            label_nb = flip_y[next_cell]
            order_me = flip_x
            order_nb = flip_x[next_cell]
        else:
            label_me = flip_x
            label_nb = flip_x[next_cell]
            order_me = flip_y
            order_nb = flip_y[next_cell]
        my_edge = jnp.bitwise_xor(global_side, 2 * label_me)
        theirs = jnp.bitwise_xor((global_side + 2) % 4, 2 * label_nb)
        edge_code = theirs + 4 * jnp.bitwise_xor(order_me, order_nb)
        elem_tab = elem_tab.at[my_edge, number].set(jnp.where(inside, number[next_cell], -1))
        edge_tab = edge_tab.at[my_edge, number].set(jnp.where(inside, edge_code, 0))
    return (elem_tab, edge_tab)


def draw_nbr_elem(key, part):
    return connect_tables(key)[0]


def draw_nbr_edge(key, part):
    return connect_tables(key)[1]


def plant(values, stream_key, smallest, largest):
    place = [jax.random.randint(jax.random.fold_in(stream_key, axis), (), 0, length) for axis, length in enumerate(values.shape)]
    longest = values.shape.index(max(values.shape))
    neighbour = place[:longest] + [(place[longest] + 1) % values.shape[longest]] + place[longest + 1:]
    return values.at[tuple(place)].set(smallest).at[tuple(neighbour)].set(largest)


def shard_levels(stream_key, shape, cuts, low, largest):
    def one(dim, parts):
        steps = jax.random.uniform(jax.random.fold_in(jax.random.fold_in(stream_key, 6), dim), (parts,), jnp.float32, low / len(cuts), largest / len(cuts))
        return jnp.repeat(jnp.exp(steps), shape[dim] // parts).reshape((-1,) + (1,) * (len(shape) - dim - 1))

    gain = one(*cuts[0])
    for cut in cuts[1:]:
        gain = gain * one(*cut)
    return gain


def setup_inputs(seed: int = 0) -> dict:
    arg_keys = jax.random.split(jax.random.key(seed), 6)
    return {
        "concentration": jnp.clip(jax.random.uniform(arg_keys[0], (NZ, NODES, ELEMS), jnp.float32, -1.0, 1.0) * shard_levels(arg_keys[0], (NZ, NODES, ELEMS), ((0, 16), (2, 8)), -0.4, 0.0), -1.0, 1.0),
        "geometry": jnp.clip(jnp.exp(math.log(2.0) - 1.3862944 * jax.random.uniform(arg_keys[1], (2, ELEMS), jnp.float32) ** shard_levels(arg_keys[1], (2, ELEMS), ((1, 8),), -0.2, 0.2)), 0.5, 2.0),
        "nbr_elem": draw_nbr_elem(jax.random.fold_in(arg_keys[5], 71), 0),
        "nbr_edge": draw_nbr_edge(jax.random.fold_in(arg_keys[5], 71), 0),
        "wall_flags": plant((jax.random.randint(arg_keys[4], (NZ,), 0, 2) < 1).astype(jnp.int32), jax.random.fold_in(arg_keys[4], 1), 0, 1),
    }


time_step = 0.2
axial_stiffness = 0.002
plane_stiffness = 1.0
edge_penalty = 4.0
axial_mobility = 0.002
mobility_floor = 0.05
highest = lax.Precision.HIGHEST

def point_tables():
    degree = 7
    points = np.arange(degree + 1)
    theta = np.pi * points / degree
    nodes_x = np.cos(theta)
    signs = np.where((points == 0) | (points == degree), 2.0, 1.0) * (-1.0) ** points
    differ = nodes_x[:, None] - nodes_x[None, :]
    deriv = np.outer(signs, 1.0 / signs) / (differ + np.eye(degree + 1))
    deriv = deriv - np.eye(degree + 1) * deriv.sum(axis=1)[:, None]
    inner = np.ones(degree - 1)
    for number in range(1, (degree - 1) // 2 + 1):
        inner = inner - 2.0 * np.cos(2 * number * theta[1:degree]) / (4 * number * number - 1)
    weights = np.zeros(degree + 1)
    weights[1:degree] = 2.0 * inner / degree
    weights[0] = 1.0 / degree ** 2
    weights[degree] = 1.0 / degree ** 2
    return (deriv, weights)

def make_tables():
    deriv, weights = point_tables()
    grad_x = np.kron(np.eye(8), deriv)
    grad_y = np.kron(deriv, np.eye(8))
    mass_w = np.kron(weights, weights)
    return (jnp.asarray(grad_x, jnp.float32), jnp.asarray(grad_y, jnp.float32), jnp.asarray(mass_w, jnp.float32), jnp.asarray(weights, jnp.float32))

def fourier_table(length):
    planes = np.arange(length)
    wave_no = (planes + 1) // 2
    phase = np.outer(wave_no, planes) % length * (2.0 * np.pi / length)
    table = np.where((planes % 2 == 1)[:, None], np.cos(phase), np.sin(phase)) * np.sqrt(2.0 / length)
    table[0] = 1.0 / np.sqrt(length)
    table[length - 1] = np.cos(phase[length - 1]) / np.sqrt(length)
    return table

def weak_flux(field, mobility, grad_x, grad_y, mass_w, jacobian, scale_x, scale_y):
    along_x = jnp.einsum('nm,ame->ane', grad_x, field, precision=highest)
    along_y = jnp.einsum('nm,ame->ane', grad_y, field, precision=highest)
    flux_x = mass_w[:, None] * mobility * along_x * (jacobian * scale_x * scale_x)
    flux_y = mass_w[:, None] * mobility * along_y * (jacobian * scale_y * scale_y)
    return jnp.einsum('mn,ame->ane', grad_x, flux_x, precision=highest) + jnp.einsum('mn,ame->ane', grad_y, flux_y, precision=highest)

def edge_traces(field):
    grid = field.reshape(field.shape[0], 8, 8, field.shape[2])
    return jnp.stack([grid[:, 0, :, :], grid[:, :, 7, :], grid[:, 7, :, :], grid[:, :, 0, :]], axis=2)

def add_edges(field, penalty):
    grid = field.reshape(field.shape[0], 8, 8, field.shape[2])
    grid = grid.at[:, 0, :, :].add(penalty[:, :, 0])
    grid = grid.at[:, :, 7, :].add(penalty[:, :, 1])
    grid = grid.at[:, 7, :, :].add(penalty[:, :, 2])
    grid = grid.at[:, :, 0, :].add(penalty[:, :, 3])
    return grid.reshape(field.shape)

def reference(concentration, geometry, nbr_elem, nbr_edge, wall_flags):
    grad_x, grad_y, mass_w, edge_w = make_tables()
    scale_x = geometry[0]
    scale_y = geometry[1]
    jacobian = 1.0 / (scale_x * scale_y)
    planes = concentration.shape[0]
    elems = concentration.shape[2]

    def plane_block(field):
        chem = field * field * field - field
        mobility = jnp.maximum(1.0 - field * field, mobility_floor)
        explicit = jacobian * mass_w[:, None] * field / time_step - weak_flux(chem, mobility, grad_x, grad_y, mass_w, jacobian, scale_x, scale_y)
        bulk = jacobian * mass_w[:, None] * chem
        return (explicit, bulk)
    explicit, bulk = lax.map(plane_block, concentration.reshape(planes // 16, 16, 64, elems))
    explicit = explicit.reshape(planes, 64, elems)
    bulk = bulk.reshape(planes, 64, elems)
    fourier = jnp.asarray(fourier_table(planes), jnp.float32)
    wave_all = ((jnp.arange(planes, dtype=jnp.int32) + 1) // 2).astype(jnp.float32)
    explicit_hat = jnp.einsum('kp,pne->kne', fourier, explicit, precision=highest)
    bulk_hat = jnp.einsum('kp,pne->kne', fourier, bulk, precision=highest)
    right_side = explicit_hat - axial_mobility * (wave_all * wave_all)[:, None, None] * bulk_hat
    wall = nbr_elem < 0
    safe_ids = jnp.maximum(nbr_elem, 0).astype(jnp.int32)
    position = (nbr_edge % 4 * elems + safe_ids).astype(jnp.int32).reshape(-1)
    reverse = nbr_edge >= 4

    def solve_block(block):
        rhs_b, wave_b, flag_b = block
        count = rhs_b.shape[0]
        mass_coef = 1.0 / time_step + axial_stiffness * wave_b * wave_b
        flag_f = flag_b.astype(jnp.float32)

        def helm_apply(field):
            result = jacobian * mass_w[:, None] * mass_coef[:, None, None] * field
            result = result + plane_stiffness * weak_flux(field, 1.0, grad_x, grad_y, mass_w, jacobian, scale_x, scale_y)
            traces = edge_traces(field)
            flat = traces.reshape(count, 8, 4 * elems)
            values = jnp.take(flat, position, axis=2).reshape(count, 8, 4, elems)
            values = jnp.where(reverse[None, None], values[:, ::-1], values)
            jump = jnp.where(wall[None, None], flag_f[:, None, None, None] * traces, traces - values)
            penalty = edge_penalty * edge_w[None, :, None, None] * jump
            return add_edges(result, penalty)
        solution = jnp.zeros_like(rhs_b)
        residual = rhs_b
        direction = rhs_b
        norm_now = lax.optimization_barrier(jnp.sum(residual * residual, axis=(1, 2)))
        for sweep in range(ITERS):
            image = helm_apply(direction)
            alpha = norm_now / lax.optimization_barrier(jnp.sum(direction * image, axis=(1, 2)))
            solution = solution + alpha[:, None, None] * direction
            residual = residual - alpha[:, None, None] * image
            if sweep + 1 < ITERS:
                norm_next = lax.optimization_barrier(jnp.sum(residual * residual, axis=(1, 2)))
                direction = residual + (norm_next / norm_now)[:, None, None] * direction
                norm_now = norm_next
        return solution
    result = lax.map(solve_block, (right_side.reshape(planes // 16, 16, 64, elems), wave_all.reshape(planes // 16, 16), wall_flags.reshape(planes // 16, 16)))
    return result.reshape(planes, 64, elems)
```

```python
import functools

import jax
import jax.numpy as jnp
import ml_dtypes
import numpy as np
from jax import lax
from jax.experimental import pallas as pl
from jax.experimental.pallas import tpu as pltpu
from jax.sharding import PartitionSpec as P

time_step = 0.2
axial_stiffness = 0.002
edge_penalty = 4.0
axial_mobility = 0.002
mobility_floor = 0.05

MESH = pl.DeviceIdType.MESH
f32 = jnp.float32
bf16 = jnp.bfloat16


def point_tables():
    degree = 7
    points = np.arange(degree + 1)
    theta = np.pi * points / degree
    nodes_x = np.cos(theta)
    signs = np.where((points == 0) | (points == degree), 2.0, 1.0) * (-1.0) ** points
    differ = nodes_x[:, None] - nodes_x[None, :]
    deriv = np.outer(signs, 1.0 / signs) / (differ + np.eye(degree + 1))
    deriv = deriv - np.eye(degree + 1) * deriv.sum(axis=1)[:, None]
    inner = np.ones(degree - 1)
    for number in range(1, (degree - 1) // 2 + 1):
        inner = inner - 2.0 * np.cos(2 * number * theta[1:degree]) / (4 * number * number - 1)
    weights = np.zeros(degree + 1)
    weights[1:degree] = 2.0 * inner / degree
    weights[0] = 1.0 / degree**2
    weights[degree] = 1.0 / degree**2
    return (deriv, weights)


def fourier_table(length):
    planes = np.arange(length)
    wave_no = (planes + 1) // 2
    phase = np.outer(wave_no, planes) % length * (2.0 * np.pi / length)
    table = np.where((planes % 2 == 1)[:, None], np.cos(phase), np.sin(phase)) * np.sqrt(
        2.0 / length
    )
    table[0] = 1.0 / np.sqrt(length)
    table[length - 1] = np.cos(phase[length - 1]) / np.sqrt(length)
    return table


def parts(matrix):
    high = matrix.astype(ml_dtypes.bfloat16)
    low = (matrix - high.astype(np.float64)).astype(ml_dtypes.bfloat16)
    return high, low


def four(matrix):
    high, low = parts(matrix)
    return np.concatenate([high, high, low, low], axis=1)


def constants():
    deriv, weights = point_tables()
    grad_x = np.kron(np.eye(8), deriv)
    grad_y = np.kron(deriv, np.eye(8))
    mass = np.kron(weights, weights)
    forward = four(np.concatenate([grad_x, grad_y], axis=0))
    back = np.concatenate([four(grad_x.T * mass), four(grad_y.T * mass)], axis=1)
    stiff_x = grad_x.T @ (mass[:, None] * grad_x)
    stiff_y = grad_y.T @ (mass[:, None] * grad_y)
    stiff = four(np.concatenate([stiff_x, stiff_y], axis=0))
    table = fourier_table(256)
    wave = (np.arange(256) + 1) // 2
    scaled = -axial_mobility * (wave * wave)[:, None] * table
    fh, fl = parts(table)
    gh, gl = parts(scaled)
    fourier = np.concatenate([fh, fh, fl, gh, gh, gl], axis=1)
    mass_b = np.broadcast_to(mass[:, None], (64, 128)).astype(np.float32)
    return forward, back, stiff, fourier, mass_b, [float(w) for w in weights]


def split(value):
    high = value.astype(bf16)
    return high, (value - high.astype(f32)).astype(bf16)


def split4(value):
    high, low = split(value)
    return jnp.concatenate([high, low, high, low], axis=0)


def dot(a, b):
    return jnp.dot(a, b, preferred_element_type=f32)


def lane_groups(shape):
    return lax.broadcasted_iota(jnp.int32, shape, 1) // 32


def swap4(x0, x1, x2, x3):
    group = lane_groups(x0.shape)
    low, even = group < 2, group % 2 == 0
    a0 = jnp.where(low, x0, pltpu.roll(x2, 64, 1))
    a2 = jnp.where(low, pltpu.roll(x0, 64, 1), x2)
    a1 = jnp.where(low, x1, pltpu.roll(x3, 64, 1))
    a3 = jnp.where(low, pltpu.roll(x1, 64, 1), x3)
    return (
        jnp.where(even, a0, pltpu.roll(a1, 32, 1)),
        jnp.where(even, pltpu.roll(a0, 96, 1), a1),
        jnp.where(even, a2, pltpu.roll(a3, 32, 1)),
        jnp.where(even, pltpu.roll(a2, 96, 1), a3),
    )


def node_of(edge, t):
    return (t, 8 * t + 7, 56 + t, 8 * t)[edge]


def kernel(
    edge_w,
    c_ref, geo_ref, nel_ref, ned_ref, flag_ref, fwd_ref, back_ref, stiff_ref, four_ref, mass_ref,
    out_ref,
    cbuf, send1, recv1, ze, zb, send2, recv2, r0, q1, q2, xbuf,
    lane_tab, src_tab, rev_tab, wall_tab, cross_tab, flag_tab, coef_tab, mc_tab,
    hsend, hrecv, dsend, drecv, scal,
    csem, s1sem, r1sem, s2sem, r2sem, hs_sem, hr_sem, ds_sem, dr_sem, osem,
):
    xy = lax.axis_index("xy")
    gz = lax.axis_index("gz")
    z, x = gz // 4, gz % 4

    def load_c(dz):
        tile = (z + dz) % 4
        return pltpu.make_async_copy(
            c_ref.at[:, :, pl.ds(pl.multiple_of(tile * 128, 128), 128)], cbuf.at[dz], csem.at[dz]
        )

    for dz in (1, 3, 0, 2):
        load_c(dz).start()

    barrier = pltpu.get_barrier_semaphore()
    for d in range(1, 16):
        pl.semaphore_signal(barrier, 1, device_id=(xy, (gz + d) % 16), device_id_type=MESH)
    for d in range(1, 8):
        pl.semaphore_signal(barrier, 1, device_id=((xy + d) % 8, gz), device_id_type=MESH)

    scale_x, scale_y = geo_ref[0:1, :], geo_ref[1:2, :]
    jac = 1.0 / (scale_x * scale_y)
    for i, row in enumerate((jac, jac * scale_x * scale_x, jac * scale_y * scale_y)):
        mine = jnp.zeros((8, 128), f32)
        for tile in range(4):
            part = jnp.broadcast_to(row[:, 128 * tile : 128 * tile + 128], (8, 128))
            coef_tab[i, tile] = part
            group = lane_groups((8, 128))
            for d in range(4):
                one = jnp.where(group == d, part, 0.0)
                one = one + pltpu.roll(one, 64, 1)
                one = one + pltpu.roll(one, 32, 1)
                mine = jnp.where((z == tile) & (x == d), one, mine)
        coef_tab[i, 4] = mine
    for a in range(4):
        for tile in range(4):
            cols = slice(128 * tile, 128 * tile + 128)
            elem = jnp.broadcast_to(nel_ref[a : a + 1, cols], (8, 128))
            code = jnp.broadcast_to(ned_ref[a : a + 1, cols], (8, 128))
            wall = elem < 0
            safe = jnp.maximum(elem, 0)
            owner = lax.shift_right_logical(safe, 9)
            local = safe & 511
            lane_tab[a, tile] = local & 127
            src_tab[a, tile] = jnp.where(
                wall, -1, jnp.where(owner == xy, (code & 3) * 4 + lax.shift_right_logical(local, 7), 16)
            )
            rev_tab[a, tile] = jnp.where(code >= 4, 1, 0)
            wall_tab[a, tile] = jnp.where(wall, 1, 0)
            cross_tab[a, tile] = jnp.where((owner != xy) & (elem >= 0), 1, 0)
    mode = lax.broadcasted_iota(jnp.int32, (16, 128), 0)
    flags = jnp.zeros((16, 128), f32)
    for k in range(16):
        flags = jnp.where(mode == k, flag_ref[k].astype(f32), flags)
    flag_tab[...] = flags
    wave = lax.shift_right_logical(mode + 16 * gz + 1, 1).astype(f32)
    mc_tab[...] = 1.0 / time_step + axial_stiffness * wave * wave

    pl.semaphore_wait(barrier, 22)

    def copy1(h, pq):
        return pltpu.make_async_remote_copy(
            send1.at[h, pq], recv1.at[gz, pq], s1sem.at[h], r1sem.at[gz],
            device_id=(xy, h), device_id_type=MESH,
        )

    def pack(s, dz):
        tile = (z + dz) % 4
        pq = s
        ys = swap4(*[cbuf[dz, 4 * pq + pr] for pr in range(4)])
        for d in range(4):
            send1[4 * tile + d, pq] = ys[d]
        for dx in range(4):
            h = 4 * tile + (x + dx) % 4

            @pl.when(h != gz)
            def _():
                copy1(h, pq).start()

    for pair in ((1, 3), (0, 2)):
        for dz in pair:
            load_c(dz).wait()

        def pack_pair(s, carry, pair=pair):
            for dz in pair:
                pack(s, dz)
            return carry

        lax.fori_loop(0, 4, pack_pair, 0)
    recv1[gz] = send1[gz]

    cj, ca, cb = (coef_tab[i, 4][0:1, :] for i in range(3))
    cj4, ca4, cb4 = (jnp.concatenate([v] * 4, axis=1) for v in (cj, ca, cb))
    mass4 = jnp.concatenate([mass_ref[...]] * 4, axis=1)

    def plane_terms(g):
        field = jnp.concatenate([recv1[g, pq] for pq in range(4)], axis=1)
        square = field * field
        chem = square * field - field
        mobility = jnp.maximum(1.0 - square, mobility_floor)
        along = dot(fwd_ref[...], split4(chem))
        flux_x = mobility * along[:64] * ca4
        flux_y = mobility * along[64:] * cb4
        both = jnp.concatenate([split4(flux_x), split4(flux_y)], axis=0)
        weak = dot(back_ref[...], both)
        weight = cj4 * mass4
        explicit = weight * field * (1.0 / time_step) - weak
        bulk = weight * chem
        for value, ref in ((explicit, ze), (bulk, zb)):
            for pq in range(4):
                cols = slice(128 * pq, 128 * pq + 128)
                for jh in range(2):
                    rows = [
                        value[8 * (4 * jh + jl) : 8 * (4 * jh + jl) + 8, cols] for jl in range(4)
                    ]
                    for pr, y in enumerate(swap4(*rows)):
                        start = (g * 16 + 4 * pq + pr) * 16 + 8 * jh
                        ref[pl.ds(pl.multiple_of(start, 8), 8), :] = y

    def from_source(s, carry):
        dz = jnp.where(s < 8, 1 + 2 * (s // 4), 2 * (s // 4 - 2))
        g = ((z + 4 - dz) % 4) * 4 + (x + 4 - s % 4) % 4

        @pl.when(g != gz)
        def _():
            pltpu.make_async_remote_copy(
                send1.at[g], recv1.at[g], s1sem.at[g], r1sem.at[g],
                device_id=(xy, g), device_id_type=MESH,
            ).wait_recv()

        plane_terms(g)
        return carry

    lax.fori_loop(0, 16, from_source, 0)

    def copy2(h, rc):
        rows = pl.ds(rc * 2, 2)
        return pltpu.make_async_remote_copy(
            send2.at[h, rows], recv2.at[gz, rows], s2sem.at[h], r2sem.at[gz],
            device_id=(xy, h), device_id_type=MESH,
        )

    offsets = (1, 4, 3, 12, 10, 5, 15, 7, 13, 2, 8, 6, 9, 14, 11)

    def transform(rc, carry):
        blocks = []
        for ref in (ze, zb):
            pair = [ref[pl.ds(2 * rc + q, 256, stride=16), :] for q in range(2)]
            high, low = split(jnp.concatenate(pair, axis=1))
            blocks += [high, low, high]
        res = dot(four_ref[...], jnp.concatenate(blocks, axis=0))
        for h in range(16):
            for q in range(2):
                send2[h, 2 * rc + q] = res[16 * h : 16 * h + 16, 128 * q : 128 * q + 128]
        for d in offsets:
            copy2((gz + d) % 16, rc).start()
        for q in range(2):
            recv2[gz, 2 * rc + q] = send2[gz, 2 * rc + q]
        return carry

    lax.fori_loop(0, 8, transform, 0)

    def settle2(d, carry):
        g = (gz + d) % 16
        pltpu.make_async_remote_copy(
            send2.at[g], recv2.at[g], s2sem.at[g], r2sem.at[g],
            device_id=(xy, g), device_id_type=MESH,
        ).wait_recv()
        return carry

    lax.fori_loop(1, 16, settle2, 0)

    recv2f = recv2.reshape(16 * 16 * 16, 128)

    def assemble(k, tile):
        for jh in range(2):
            xs = [
                recv2f[pl.ds(((4 * tile + s) * 16 + 8 * jh) * 16 + k, 8, stride=16), :]
                for s in range(4)
            ]
            for jl, y in enumerate(swap4(*xs)):
                start = (tile * 16 + k) * 64 + (4 * jh + jl) * 8
                r0[pl.ds(pl.multiple_of(start, 8), 8), :] = y

    def interior(src, dst, tile, kq):
        rows = [pl.ds(pl.multiple_of((tile * 16 + 4 * kq + s) * 64, 64), 64) for s in range(4)]
        field = jnp.concatenate([src[r, :] for r in rows], axis=1)
        res = dot(stiff_ref[...], split4(field))
        cj_t, ca_t, cb_t = (coef_tab[i, tile][0:1, :] for i in range(3))
        weight = mass_ref[...] * cj_t
        for s in range(4):
            cols = slice(128 * s, 128 * s + 128)
            mc = mc_tab[pl.ds(4 * kq + s, 1), :]
            dst[rows[s], :] = (
                weight * mc * field[:, cols] + ca_t * res[:64, cols] + cb_t * res[64:, cols]
            )

    def first_pass(s, carry):
        tile, kq = s // 4, s % 4
        for k in range(4):
            assemble(4 * kq + k, tile)
        interior(r0, q1, tile, kq)
        return carry

    lax.fori_loop(0, 16, first_pass, 0)

    def second_pass(s, carry):
        interior(q1, q2, s // 4, s % 4)
        return carry

    def trace(ref, tile, edge, t):
        return ref[pl.ds(tile * 1024 + node_of(edge, t), 16, stride=64), :]

    def halo_copy(which, side):
        peer = (xy + (7, 1)[side]) % 8
        return pltpu.make_async_remote_copy(
            hsend.at[which, side], hrecv.at[which, side],
            hs_sem.at[which, side], hr_sem.at[which, side],
            device_id=(peer, gz), device_id_type=MESH,
        )

    def send_halo(ref, which):
        for side, tile in ((0, 0), (1, 3)):

            def fill(t, carry, side=side, tile=tile):
                value = jnp.zeros((16, 128), f32)
                for a in range(4):
                    on = jnp.concatenate([cross_tab[a, tile]] * 2, axis=0) > 0
                    value = jnp.where(on, trace(ref, tile, a, t), value)
                hsend[which, side, t] = value
                return carry

            lax.fori_loop(0, 8, fill, 0)
            halo_copy(which, side).start()

    def penalize(src, dst, which):
        for side in range(2):
            halo_copy(which, side).wait_recv()
        first = lax.broadcasted_iota(jnp.int32, (16, 128), 1) < 64
        flag = flag_tab[...]

        def one(s, carry):
            tp, tile = s // 4, s % 4
            ts = (tp, 7 - tp)
            weight = jnp.where(
                tp == 0, edge_w[0], jnp.where(tp == 1, edge_w[1], jnp.where(tp == 2, edge_w[2], edge_w[3]))
            ) * edge_penalty
            for a in range(4):
                two = lambda tab: jnp.concatenate([tab[a, tile]] * 2, axis=0)
                lane, source, rev, wall = (two(t) for t in (lane_tab, src_tab, rev_tab, wall_tab))
                rev, wall = rev > 0, wall > 0
                got = [jnp.zeros((16, 128), f32) for _ in ts]
                for b in range(4):
                    for tile_b in range(4):
                        here = source == 4 * b + tile_b
                        for i, t in enumerate(ts):
                            picked = jnp.take_along_axis(trace(src, tile_b, b, t), lane, axis=1)
                            got[i] = jnp.where(here, picked, got[i])
                here = source == 16
                for i, t in enumerate(ts):
                    side = jnp.where(first, hrecv[which, 0, t], hrecv[which, 1, t])
                    picked = jnp.take_along_axis(side, lane, axis=1)
                    got[i] = jnp.where(here, picked, got[i])
                other = [jnp.where(rev, got[1 - i], got[i]) for i in range(2)]
                factor = jnp.where(wall, flag, 1.0)
                for i, t in enumerate(ts):
                    pen = weight * (factor * trace(src, tile, a, t) - other[i])
                    at = pl.ds(tile * 1024 + node_of(a, t), 16, stride=64)
                    dst[at, :] = dst[at, :] + pen
            return carry

        lax.fori_loop(0, 16, one, 0)

    def total(which, n):
        for d in range(1, 8):
            pltpu.make_async_remote_copy(
                dsend.at[which], drecv.at[which, xy], ds_sem.at[which, (xy + d) % 8],
                dr_sem.at[which, xy], device_id=((xy + d) % 8, gz), device_id_type=MESH,
            ).start()
        drecv[which, xy] = dsend[which]

    def total_done(which, n):
        for d in range(1, 8):
            g = (xy + d) % 8
            pltpu.make_async_remote_copy(
                dsend.at[which], drecv.at[which, g], ds_sem.at[which, g],
                dr_sem.at[which, g], device_id=(g, gz), device_id_type=MESH,
            ).wait_recv()
        out = []
        for i in range(n):
            acc = drecv[which, 0, i]
            for g in range(1, 8):
                acc = acc + drecv[which, g, i]
            out.append(jnp.broadcast_to(jnp.sum(acc, axis=1, keepdims=True), (16, 128)))
        return out

    def rows_of(tile, k):
        return pl.ds(pl.multiple_of((tile * 16 + k) * 64, 64), 64)

    def sum8(value):
        return jnp.sum(value, axis=0, keepdims=True)

    send_halo(r0, 0)
    penalize(r0, q1, 0)
    send_halo(q1, 1)

    def dots1(k, carry):
        rr = jnp.zeros((64, 128), f32)
        pq = jnp.zeros((64, 128), f32)
        for tile in range(4):
            a, b = r0[rows_of(tile, k), :], q1[rows_of(tile, k), :]
            rr, pq = rr + a * a, pq + a * b
        dsend[0, 0, pl.ds(k, 1), :] = sum8(rr)
        dsend[0, 1, pl.ds(k, 1), :] = sum8(pq)
        return carry

    lax.fori_loop(0, 16, dots1, 0)
    total(0, 2)
    lax.fori_loop(0, 16, second_pass, 0)
    penalize(q1, q2, 1)
    rr0, pq0 = total_done(0, 2)
    scal[0] = rr0 / pq0

    def dots2(k, carry):
        accs = [jnp.zeros((64, 128), f32) for _ in range(3)]
        alpha = scal[0, pl.ds(k, 1), :]
        for tile in range(4):
            rows = rows_of(tile, k)
            u, v = r0[rows, :], q1[rows, :]
            r1 = u - alpha * v
            s = v - alpha * q2[rows, :]
            for i, term in enumerate((r1 * r1, r1 * s, r1 * v + u * s)):
                accs[i] = accs[i] + term
        for i in range(3):
            dsend[1, i, pl.ds(k, 1), :] = sum8(accs[i])
        return carry

    lax.fori_loop(0, 16, dots2, 0)
    total(1, 3)
    rr1, r1s, cross = total_done(1, 3)
    alpha0 = rr0 / pq0
    beta = rr1 / rr0
    alpha1 = rr1 / (r1s + beta * cross + beta * beta * pq0)
    scal[1] = alpha0 + alpha1 * (1.0 + beta)
    scal[2] = alpha1 * alpha0

    def finish(tile, carry):
        def one(k, carry):
            rows = rows_of(tile, k)
            xbuf[tile, k] = (
                scal[1, pl.ds(k, 1), :] * r0[rows, :] - scal[2, pl.ds(k, 1), :] * q1[rows, :]
            )
            return carry

        lax.fori_loop(0, 16, one, 0)
        out_copy(tile).start()
        return carry

    def out_copy(tile):
        return pltpu.make_async_copy(
            xbuf.at[tile],
            out_ref.at[:, :, pl.ds(pl.multiple_of(tile * 128, 128), 128)],
            osem.at[tile],
        )

    lax.fori_loop(0, 4, finish, 0)

    def sent(d, carry):
        g = (gz + d) % 16
        for buf, dst, ssem, rsem in ((send1, recv1, s1sem, r1sem), (send2, recv2, s2sem, r2sem)):
            pltpu.make_async_remote_copy(
                buf.at[g], dst.at[g], ssem.at[g], rsem.at[g], device_id=(xy, g), device_id_type=MESH
            ).wait_send()
        return carry

    lax.fori_loop(1, 16, sent, 0)
    for which in range(2):
        for side in range(2):
            halo_copy(which, side).wait_send()
        for d in range(1, 8):
            g = (xy + d) % 8
            pltpu.make_async_remote_copy(
                dsend.at[which], drecv.at[which, g], ds_sem.at[which, g],
                dr_sem.at[which, g], device_id=(g, gz), device_id_type=MESH,
            ).wait_send()
    for tile in range(4):
        out_copy(tile).wait()


def per_device(concentration, geometry, nbr_elem, nbr_edge, wall_flags):
    forward, back, stiff, fourier, mass_b, edge_w = constants()
    vmem = pl.BlockSpec(memory_space=pltpu.VMEM)
    dma = pltpu.SemaphoreType.DMA
    V = pltpu.VMEM
    i32 = jnp.int32
    return pl.pallas_call(
        functools.partial(kernel, edge_w),
        out_shape=jax.ShapeDtypeStruct(concentration.shape, f32),
        in_specs=[pl.BlockSpec(memory_space=pl.ANY), vmem, vmem, vmem, pl.BlockSpec(memory_space=pltpu.SMEM)]
        + [vmem] * 5,
        out_specs=pl.BlockSpec(memory_space=pl.ANY),
        scratch_shapes=[
            V((4, 16, 64, 128), f32),
            V((16, 4, 64, 128), f32),
            V((16, 4, 64, 128), f32),
            V((4096, 128), f32),
            V((4096, 128), f32),
            V((16, 16, 16, 128), f32),
            V((16, 16, 16, 128), f32),
            V((4096, 128), f32),
            V((4096, 128), f32),
            V((4096, 128), f32),
            V((4, 16, 64, 128), f32),
            V((4, 4, 8, 128), i32),
            V((4, 4, 8, 128), i32),
            V((4, 4, 8, 128), i32),
            V((4, 4, 8, 128), i32),
            V((4, 4, 8, 128), i32),
            V((16, 128), f32),
            V((3, 5, 8, 128), f32),
            V((16, 128), f32),
            V((2, 2, 8, 16, 128), f32),
            V((2, 2, 8, 16, 128), f32),
            V((2, 3, 16, 128), f32),
            V((2, 8, 3, 16, 128), f32),
            V((3, 16, 128), f32),
            dma((4,)),
            dma((16,)),
            dma((16,)),
            dma((16,)),
            dma((16,)),
            dma((2, 2)),
            dma((2, 2)),
            dma((2, 8)),
            dma((2, 8)),
            dma((4,)),
        ],
        compiler_params=pltpu.CompilerParams(
            collective_id=0, has_side_effects=True, vmem_limit_bytes=50 << 20
        ),
    )(
        concentration, geometry, nbr_elem, nbr_edge, wall_flags,
        jnp.asarray(forward), jnp.asarray(back), jnp.asarray(stiff), jnp.asarray(fourier),
        jnp.asarray(mass_b),
    )


def solution(mesh):
    return jax.shard_map(
        per_device,
        mesh=mesh,
        in_specs=(P("gz", None, "xy"), P(None, "xy"), P(None, "xy"), P(None, "xy"), P("gz")),
        out_specs=P("gz", None, "xy"),
        check_vma=False,
    )
```

```python
import functools

import jax
import jax.numpy as jnp
import ml_dtypes
import numpy as np
from jax import lax
from jax.experimental import pallas as pl
from jax.experimental.pallas import tpu as pltpu
from jax.sharding import PartitionSpec as P

time_step = 0.2
axial_stiffness = 0.002
edge_penalty = 4.0
axial_mobility = 0.002
mobility_floor = 0.05

MESH = pl.DeviceIdType.MESH
f32 = jnp.float32
bf16 = jnp.bfloat16


def point_tables():
    degree = 7
    points = np.arange(degree + 1)
    theta = np.pi * points / degree
    nodes_x = np.cos(theta)
    signs = np.where((points == 0) | (points == degree), 2.0, 1.0) * (-1.0) ** points
    differ = nodes_x[:, None] - nodes_x[None, :]
    deriv = np.outer(signs, 1.0 / signs) / (differ + np.eye(degree + 1))
    deriv = deriv - np.eye(degree + 1) * deriv.sum(axis=1)[:, None]
    inner = np.ones(degree - 1)
    for number in range(1, (degree - 1) // 2 + 1):
        inner = inner - 2.0 * np.cos(2 * number * theta[1:degree]) / (4 * number * number - 1)
    weights = np.zeros(degree + 1)
    weights[1:degree] = 2.0 * inner / degree
    weights[0] = 1.0 / degree**2
    weights[degree] = 1.0 / degree**2
    return (deriv, weights)


def fourier_table(length):
    planes = np.arange(length)
    wave_no = (planes + 1) // 2
    phase = np.outer(wave_no, planes) % length * (2.0 * np.pi / length)
    table = np.where((planes % 2 == 1)[:, None], np.cos(phase), np.sin(phase)) * np.sqrt(
        2.0 / length
    )
    table[0] = 1.0 / np.sqrt(length)
    table[length - 1] = np.cos(phase[length - 1]) / np.sqrt(length)
    return table


def parts(matrix):
    high = matrix.astype(ml_dtypes.bfloat16)
    low = (matrix - high.astype(np.float64)).astype(ml_dtypes.bfloat16)
    return high, low


def four(matrix):
    high, low = parts(matrix)
    return np.concatenate([high, high, low, low], axis=1)


def constants():
    deriv, weights = point_tables()
    grad_x = np.kron(np.eye(8), deriv)
    grad_y = np.kron(deriv, np.eye(8))
    mass = np.kron(weights, weights)
    forward = four(np.concatenate([grad_x, grad_y], axis=0))
    back = np.concatenate([four(grad_x.T * mass), four(grad_y.T * mass)], axis=1)
    table = fourier_table(256)
    wave = (np.arange(256) + 1) // 2
    scaled = -axial_mobility * (wave * wave)[:, None] * table
    fh, fl = parts(table)
    gh, gl = parts(scaled)
    fourier = np.concatenate([fh, fh, fl, gh, gh, gl], axis=1)
    mass_b = np.broadcast_to(mass[:, None], (64, 128)).astype(np.float32)
    line = deriv.T @ (weights[:, None] * deriv)
    return forward, back, fourier, mass_b, weights, line


def split(value):
    high = value.astype(bf16)
    return high, (value - high.astype(f32)).astype(bf16)


def split4(value):
    high, low = split(value)
    return jnp.concatenate([high, low, high, low], axis=0)


def dot(a, b):
    return jnp.dot(a, b, preferred_element_type=f32)


def lane_groups(shape):
    return lax.broadcasted_iota(jnp.int32, shape, 1) // 32


def swap4(x0, x1, x2, x3):
    group = lane_groups(x0.shape)
    low, even = group < 2, group % 2 == 0
    a0 = jnp.where(low, x0, pltpu.roll(x2, 64, 1))
    a2 = jnp.where(low, pltpu.roll(x0, 64, 1), x2)
    a1 = jnp.where(low, x1, pltpu.roll(x3, 64, 1))
    a3 = jnp.where(low, pltpu.roll(x1, 64, 1), x3)
    return (
        jnp.where(even, a0, pltpu.roll(a1, 32, 1)),
        jnp.where(even, pltpu.roll(a0, 96, 1), a1),
        jnp.where(even, a2, pltpu.roll(a3, 32, 1)),
        jnp.where(even, pltpu.roll(a2, 96, 1), a3),
    )


def node_of(edge, t):
    return (t, 8 * t + 7, 56 + t, 8 * t)[edge]


def apply_line(line, us):
    even = [us[m] + us[7 - m] for m in range(4)]
    odd = [us[m] - us[7 - m] for m in range(4)]
    out = [None] * 8
    for i in range(4):
        e = o = None
        for m in range(4):
            ce = float(0.5 * (line[i, m] + line[i, 7 - m]))
            co = float(0.5 * (line[i, m] - line[i, 7 - m]))
            e = ce * even[m] if e is None else e + ce * even[m]
            o = co * odd[m] if o is None else o + co * odd[m]
        out[i], out[7 - i] = e + o, e - o
    return out


def kernel(
    weights, line,
    c_ref, geo_hbm, nel_hbm, ned_hbm, flag_hbm, fwd_hbm, back_hbm, four_hbm, mass_hbm,
    out_ref,
    geo_ref, nel_ref, ned_ref, flag_ref, fwd_ref, back_ref, four_ref, mass_ref,
    cbuf, send1, recv1, ze, zb, send2, recv2, r0, q1, q2, rt, qt,
    lane_tab, src_tab, rev_tab, wall_tab, cross_tab, flag_tab, coef_tab, mc_tab,
    hsend, hrecv, dsend, drecv,
    csem, isem, s1sem, r1sem, s2sem, r2sem, hs_sem, hr_sem, ds_sem, dr_sem,
):
    xy = lax.axis_index("xy")
    gz = lax.axis_index("gz")
    z, x = gz // 4, gz % 4
    PHASES = ((1, 1), (1, 0), (0, 1), (0, 0))

    def tile_of(phase):
        return 2 * ((z + phase[0]) % 2) + (x + phase[1]) % 2

    def device_at(tile, d):
        return 4 * (2 * (d // 2) + tile // 2) + 2 * (d % 2) + tile % 2

    def d_of(j):
        return 2 * ((z // 2 + j // 2) % 2) + (x // 2 + j) % 2

    def load_c(i):
        tile = tile_of(PHASES[i])
        return pltpu.make_async_copy(
            c_ref.at[:, :, pl.ds(pl.multiple_of(tile * 128, 128), 128)], cbuf.at[i], csem.at[i]
        )

    for i in range(4):
        load_c(i).start()

    barrier = pltpu.get_barrier_semaphore()
    for d in range(1, 16):
        pl.semaphore_signal(barrier, 1, device_id=(xy, (gz + d) % 16), device_id_type=MESH)
    for d in range(1, 8):
        pl.semaphore_signal(barrier, 1, device_id=((xy + d) % 8, gz), device_id_type=MESH)

    loads = [
        pltpu.make_async_copy(src, dst, isem.at[i])
        for i, (src, dst) in enumerate(
            (
                (geo_hbm, geo_ref), (nel_hbm, nel_ref), (ned_hbm, ned_ref), (flag_hbm, flag_ref),
                (fwd_hbm, fwd_ref), (back_hbm, back_ref), (mass_hbm, mass_ref), (four_hbm, four_ref),
            )
        )
    ]
    for load in loads:
        load.start()

    for i in range(4):
        load_c(i).wait()

        def pack(pq, carry, i=i):
            tile = tile_of(PHASES[i])
            ys = swap4(*[cbuf[i, 4 * pq + pr] for pr in range(4)])
            for d in range(4):
                send1[device_at(tile, d), pq] = ys[d]
            return carry

        lax.fori_loop(0, 4, pack, 0)
    recv1[gz] = send1[gz]

    for load in loads:
        load.wait()
    scale_x, scale_y = geo_ref[0:1, :], geo_ref[1:2, :]
    jac = 1.0 / (scale_x * scale_y)
    my_tile, my_d = tile_of((0, 0)), d_of(0)
    for i, row in enumerate((jac, jac * scale_x * scale_x, jac * scale_y * scale_y)):
        mine = jnp.zeros((8, 128), f32)
        for tile in range(4):
            part = jnp.broadcast_to(row[:, 128 * tile : 128 * tile + 128], (8, 128))
            coef_tab[i, tile] = part
            group = lane_groups((8, 128))
            for d in range(4):
                one = jnp.where(group == d, part, 0.0)
                one = one + pltpu.roll(one, 64, 1)
                one = one + pltpu.roll(one, 32, 1)
                mine = jnp.where((my_tile == tile) & (my_d == d), one, mine)
        coef_tab[i, 4] = mine
    for a in range(4):
        for tile in range(4):
            cols = slice(128 * tile, 128 * tile + 128)
            elem = jnp.broadcast_to(nel_ref[a : a + 1, cols], (8, 128))
            code = jnp.broadcast_to(ned_ref[a : a + 1, cols], (8, 128))
            wall = elem < 0
            safe = jnp.maximum(elem, 0)
            owner = lax.shift_right_logical(safe, 9)
            local = safe & 511
            lane_tab[a, tile] = local & 127
            src_tab[a, tile] = jnp.where(
                wall, -1, jnp.where(owner == xy, (code & 3) * 4 + lax.shift_right_logical(local, 7), 16)
            )
            rev_tab[a, tile] = jnp.where(code >= 4, 1, 0)
            wall_tab[a, tile] = jnp.where(wall, 1, 0)
            cross_tab[a, tile] = jnp.where((owner != xy) & (elem >= 0), 1, 0)
    sub = lax.broadcasted_iota(jnp.int32, (8, 128), 0)
    for kh in range(2):
        flags = jnp.zeros((8, 128), f32)
        for k in range(8):
            flags = jnp.where(sub == k, flag_ref[8 * kh + k].astype(f32), flags)
        flag_tab[kh] = flags
        wave = lax.shift_right_logical(sub + 8 * kh + 16 * gz + 1, 1).astype(f32)
        mc_tab[kh] = 1.0 / time_step + axial_stiffness * wave * wave

    def source(s):
        a, b = 1 - s // 8, 1 - (s // 4) % 2
        return device_at(2 * ((z + a) % 2) + (x + b) % 2, d_of(s % 4))

    pl.semaphore_wait(barrier, 22)

    def copy1(h, pq):
        return pltpu.make_async_remote_copy(
            send1.at[h, pq], recv1.at[gz, pq], s1sem.at[h], r1sem.at[gz],
            device_id=(xy, h), device_id_type=MESH,
        )

    def block1(g):
        return pltpu.make_async_remote_copy(
            send1.at[g], recv1.at[g], s1sem.at[g], r1sem.at[g],
            device_id=(xy, g), device_id_type=MESH,
        )

    def others(i, act):
        def one(j, carry):
            h = source(4 * i + j)

            @pl.when(h != gz)
            def _():
                act(h)

            return carry

        lax.fori_loop(0, 4, one, 0)

    def issue1(i):
        for pq in range(4):
            others(i, lambda h, pq=pq: copy1(h, pq).start())

    issue1(0)
    issue1(1)

    cj, ca, cb = (coef_tab[i, 4][0:1, :] for i in range(3))
    cj4, ca4, cb4 = (jnp.concatenate([v] * 4, axis=1) for v in (cj, ca, cb))
    mass4 = jnp.concatenate([mass_ref[...]] * 4, axis=1)

    def plane_terms(g):
        field = jnp.concatenate([recv1[g, pq] for pq in range(4)], axis=1)
        square = field * field
        chem = square * field - field
        mobility = jnp.maximum(1.0 - square, mobility_floor)
        along = dot(fwd_ref[...], split4(chem))
        flux_x = mobility * along[:64] * ca4
        flux_y = mobility * along[64:] * cb4
        both = jnp.concatenate([split4(flux_x), split4(flux_y)], axis=0)
        weak = dot(back_ref[...], both)
        weight = cj4 * mass4
        explicit = weight * field * (1.0 / time_step) - weak
        bulk = weight * chem
        for value, ref in ((explicit, ze), (bulk, zb)):
            for pq in range(4):
                cols = slice(128 * pq, 128 * pq + 128)
                for jh in range(2):
                    rows = [
                        value[8 * (4 * jh + jl) : 8 * (4 * jh + jl) + 8, cols] for jl in range(4)
                    ]
                    for pr, y in enumerate(swap4(*rows)):
                        start = (g * 16 + 4 * pq + pr) * 16 + 8 * jh
                        ref[pl.ds(pl.multiple_of(start, 8), 8), :] = y

    plane_terms(gz)

    def phase1(i, carry):
        others(i, lambda h: block1(h).wait_send())

        @pl.when(i < 2)
        def _():
            issue1(i + 2)

        def take(g):
            block1(g).wait_recv()
            plane_terms(g)

        others(i, take)
        return carry

    lax.fori_loop(0, 4, phase1, 0)

    def copy2(h, kh, which, start, size):
        rows = pl.ds(start, size)
        return pltpu.make_async_remote_copy(
            send2.at[h, kh, rows], recv2.at[gz, kh, rows], s2sem.at[h, which], r2sem.at[gz, kh],
            device_id=(xy, h), device_id_type=MESH,
        )

    def transform(rc, carry):
        blocks = []
        for ref in (ze, zb):
            pair = [ref[pl.ds(2 * rc + q, 256, stride=16), :] for q in range(2)]
            high, low = split(jnp.concatenate(pair, axis=1))
            blocks += [high, low, high]
        res = dot(four_ref[...], jnp.concatenate(blocks, axis=0))
        for h in range(16):
            for kh in range(2):
                for q in range(2):
                    row = 16 * h + 8 * kh
                    send2[h, kh, 2 * rc + q] = res[row : row + 8, 128 * q : 128 * q + 128]
        which = rc // 6
        for i in range(4):
            for j in range(4):
                if PHASES[i] == (0, 0) and j == 0:
                    continue
                copy2(device_at(tile_of(PHASES[i]), d_of(j)), 0, which, 2 * rc, 2).start()
        return carry

    lax.fori_loop(0, 8, transform, 0)
    recv2[gz] = send2[gz]

    DEPTH = 3

    def portion(p, act):
        others(p // 4, lambda h: act(copy2(h, 1, 2 + p % 4, 4 * (p % 4), 4)))

    def pump(p):
        pass

    def early(i, carry):
        others(i, lambda h: copy2(h, 0, 0, 0, 12).wait_send())
        return carry

    lax.fori_loop(0, 4, early, 0)
    for p in range(8):
        portion(p, lambda copy: copy.start())

    def arrived(kh, i):
        others(
            i,
            lambda g: pltpu.make_async_remote_copy(
                send2.at[g, kh], recv2.at[g, kh], s2sem.at[g, kh], r2sem.at[g, kh],
                device_id=(xy, g), device_id_type=MESH,
            ).wait_recv(),
        )

    def assemble(kh, tile):
        devices = [device_at(tile, d) for d in range(4)]
        for r in range(16):
            xs = [recv2[g, kh, r] for g in devices]
            for jl, y in enumerate(swap4(*xs)):
                r0[kh, tile, 32 * (r // 8) + 8 * jl + r % 8] = y

    def interior(src, dst, kh, tile):
        cj_t, ca_t, cb_t = (coef_tab[i, tile] for i in range(3))
        cjm = cj_t * mc_tab[kh]
        for j in range(8):
            us = [src[kh, tile, 8 * j + i] for i in range(8)]
            cjw, caw = cjm * float(weights[j]), ca_t * float(weights[j])
            for i, value in enumerate(apply_line(line, us)):
                dst[kh, tile, 8 * j + i] = caw * value + (cjw * float(weights[i])) * us[i]
        for i in range(8):
            us = [src[kh, tile, 8 * j + i] for j in range(8)]
            cbw = cb_t * float(weights[i])
            for j, value in enumerate(apply_line(line, us)):
                dst[kh, tile, 8 * j + i] = dst[kh, tile, 8 * j + i] + cbw * value

    def first_pass(kh):
        def one(i, carry):
            arrived(kh, i)
            if kh == 0:

                @pl.when(i % 2 == 1)
                def _():
                    pump(3 + i // 2)

            tile = 2 * ((z + 1 - i // 2) % 2) + (x + 1 - i % 2) % 2
            assemble(kh, tile)
            interior(r0, q1, kh, tile)
            return carry

        lax.fori_loop(0, 4, one, 0)

    def second_pass(kh):
        def one(tile, carry):
            interior(q1, q2, kh, tile)
            return carry

        lax.fori_loop(0, 4, one, 0)

    def halo_copy(which, side):
        peer = (xy + (7, 1)[side]) % 8
        return pltpu.make_async_remote_copy(
            hsend.at[which, side], hrecv.at[which, side],
            hs_sem.at[which, side], hr_sem.at[which, side],
            device_id=(peer, gz), device_id_type=MESH,
        )

    def send_halo(ref, kh, which):
        for side, tile in ((0, 0), (1, 3)):
            on = [cross_tab[a, tile] > 0 for a in range(4)]
            for t in range(8):
                value = jnp.zeros((8, 128), f32)
                for a in range(4):
                    value = jnp.where(on[a], ref[kh, tile, node_of(a, t)], value)
                hsend[which, side, t] = value
            halo_copy(which, side).start()

    def pick(value, lane):
        return jnp.take_along_axis(value, lane, axis=1, mode="promise_in_bounds")

    def penalize(src, dst, kh, first_portion):
        def one(tile, carry):
            if kh == 0:
                pump(first_portion + tile)
            flag = flag_tab[kh]
            for a in range(4):
                lane, src_id = lane_tab[a, tile], src_tab[a, tile]
                rev, wall = rev_tab[a, tile] > 0, wall_tab[a, tile] > 0
                factor = jnp.where(wall, flag, 1.0)
                for tp in range(4):
                    ts = (tp, 7 - tp)
                    weight = edge_penalty * float(weights[tp])
                    got = [jnp.zeros((8, 128), f32) for _ in ts]
                    for b in range(4):
                        for tile_b in range(4):
                            here = src_id == 4 * b + tile_b
                            for i, t in enumerate(ts):
                                picked = pick(src[kh, tile_b, node_of(b, t)], lane)
                                got[i] = jnp.where(here, picked, got[i])
                    for i, t in enumerate(ts):
                        at = node_of(a, t)
                        other = jnp.where(rev, got[1 - i], got[i])
                        pen = weight * (factor * src[kh, tile, at] - other)
                        dst[kh, tile, at] = dst[kh, tile, at] + pen
            return carry

        lax.fori_loop(0, 4, one, 0)

    def penalize_halo(dst, kh, which):
        for side in range(2):
            halo_copy(which, side).wait_recv()

        for tile, side in ((0, 1), (3, 0)):
            for a in range(4):
                lane, here = lane_tab[a, tile], src_tab[a, tile] == 16
                rev = rev_tab[a, tile] > 0
                for tp in range(4):
                    ts = (tp, 7 - tp)
                    weight = edge_penalty * float(weights[tp])
                    got = [pick(hrecv[which, side, t], lane) for t in ts]
                    for i, t in enumerate(ts):
                        at = node_of(a, t)
                        other = jnp.where(rev, got[1 - i], got[i])
                        dst[kh, tile, at] = dst[kh, tile, at] - jnp.where(here, weight * other, 0.0)

    def part_copy(which, g):
        return pltpu.make_async_remote_copy(
            dsend.at[which], drecv.at[which, xy], ds_sem.at[which, g], dr_sem.at[which, xy],
            device_id=(g, gz), device_id_type=MESH,
        )

    def total(which):
        for d in range(1, 8):
            part_copy(which, (xy + d) % 8).start()
        drecv[which, xy] = dsend[which]

    def total_done(which, n):
        for d in range(1, 8):
            g = (xy + d) % 8
            pltpu.make_async_remote_copy(
                dsend.at[which], drecv.at[which, g], ds_sem.at[which, g],
                dr_sem.at[which, g], device_id=(g, gz), device_id_type=MESH,
            ).wait_recv()
        out = []
        for i in range(n):
            acc = drecv[which, 0, i]
            for g in range(1, 8):
                acc = acc + drecv[which, g, i]
            out.append(jnp.broadcast_to(jnp.sum(acc, axis=1, keepdims=True), (8, 128)))
        return out

    def dots(which, n, terms):
        def one(tile, accs):
            accs = list(accs)
            for i in range(64):
                for m, term in enumerate(terms(tile, i)):
                    accs[2 * m + i % 2] = accs[2 * m + i % 2] + term
            return tuple(accs)

        accs = lax.fori_loop(0, 4, one, tuple(jnp.zeros((8, 128), f32) for _ in range(2 * n)))
        for m in range(n):
            dsend[which, m] = accs[2 * m] + accs[2 * m + 1]
        total(which)

    def solve(kh):
        first_pass(kh)
        if kh == 0:
            for p in range(8, 16):
                portion(p, lambda copy: copy.start())
        send_halo(r0, kh, 2 * kh)
        penalize(r0, q1, kh, 5)
        penalize_halo(q1, kh, 2 * kh)
        send_halo(q1, kh, 2 * kh + 1)

        def terms1(tile, n):
            u, v = r0[kh, tile, n], q1[kh, tile, n]
            return u * u, u * v

        dots(2 * kh, 2, terms1)
        if kh == 0:
            pump(9)
        second_pass(kh)
        if kh == 0:
            pump(10)
        penalize(q1, q2, kh, 11)
        penalize_halo(q2, kh, 2 * kh + 1)
        rr0, pq0 = total_done(2 * kh, 2)
        alpha0 = rr0 / pq0

        def terms2(tile, n):
            u, v = r0[kh, tile, n], q1[kh, tile, n]
            r1 = u - alpha0 * v
            s = v - alpha0 * q2[kh, tile, n]
            return r1 * r1, r1 * s, r1 * v + u * s

        dots(2 * kh + 1, 3, terms2)
        if kh == 0:
            pump(15)
        return rr0, pq0

    def conclude(kh, rr0, pq0):
        def turn(tile, carry):
            for ref, out in ((r0, rt), (q1, qt)):
                rows = ref.reshape(2 * 4 * 64 * 8, 128)
                for j in range(8):
                    for k in range(8):
                        start = ((kh * 4 + tile) * 64 + 8 * j) * 8 + k
                        out[tile, k, 8 * j : 8 * j + 8, :] = rows[pl.ds(start, 8, stride=8), :]
            return carry

        lax.fori_loop(0, 4, turn, 0)
        rr1, r1s, cross = total_done(2 * kh + 1, 3)
        alpha0 = rr0 / pq0
        beta = rr1 / rr0
        alpha1 = rr1 / (r1s + beta * cross + beta * beta * pq0)
        along_r = alpha0 + alpha1 * (1.0 + beta)
        along_q = alpha1 * alpha0

        for tile in range(4):
            for k in range(8):
                out_ref[8 * kh + k, :, 128 * tile : 128 * tile + 128] = (
                    along_r[k : k + 1] * rt[tile, k] - along_q[k : k + 1] * qt[tile, k]
                )

    first_half = solve(0)
    second_half = solve(1)
    conclude(0, *first_half)
    conclude(1, *second_half)

    def sent(i, carry):
        others(i, lambda h: copy2(h, 0, 1, 12, 4).wait_send())
        return carry

    lax.fori_loop(0, 4, sent, 0)
    for p in range(16):
        portion(p, lambda copy: copy.wait_send())
    for which in range(4):
        for side in range(2):
            halo_copy(which, side).wait_send()
        for d in range(1, 8):
            part_copy(which, (xy + d) % 8).wait_send()


def per_device(concentration, geometry, nbr_elem, nbr_edge, wall_flags):
    forward, back, fourier, mass_b, weights, line = constants()
    dma = pltpu.SemaphoreType.DMA
    V = pltpu.VMEM
    i32 = jnp.int32
    anywhere = pl.BlockSpec(memory_space=pl.ANY)
    return pl.pallas_call(
        functools.partial(kernel, weights, line),
        out_shape=jax.ShapeDtypeStruct(concentration.shape, f32),
        in_specs=[anywhere] * 9,
        out_specs=pl.BlockSpec(memory_space=pltpu.VMEM),
        scratch_shapes=[
            V((2, 512), f32),
            V((4, 512), i32),
            V((4, 512), i32),
            pltpu.SMEM((16,), i32),
            V(forward.shape, bf16),
            V(back.shape, bf16),
            V(fourier.shape, bf16),
            V((64, 128), f32),
            V((4, 16, 64, 128), f32),
            V((16, 4, 64, 128), f32),
            V((16, 4, 64, 128), f32),
            V((4096, 128), f32),
            V((4096, 128), f32),
            V((16, 2, 16, 8, 128), f32),
            V((16, 2, 16, 8, 128), f32),
            V((2, 4, 64, 8, 128), f32),
            V((2, 4, 64, 8, 128), f32),
            V((2, 4, 64, 8, 128), f32),
            V((4, 8, 64, 128), f32),
            V((4, 8, 64, 128), f32),
            V((4, 4, 8, 128), i32),
            V((4, 4, 8, 128), i32),
            V((4, 4, 8, 128), i32),
            V((4, 4, 8, 128), i32),
            V((4, 4, 8, 128), i32),
            V((2, 8, 128), f32),
            V((3, 5, 8, 128), f32),
            V((2, 8, 128), f32),
            V((4, 2, 8, 8, 128), f32),
            V((4, 2, 8, 8, 128), f32),
            V((4, 3, 8, 128), f32),
            V((4, 8, 3, 8, 128), f32),
            dma((4,)),
            dma((8,)),
            dma((16,)),
            dma((16,)),
            dma((16, 6)),
            dma((16, 2)),
            dma((4, 2)),
            dma((4, 2)),
            dma((4, 8)),
            dma((4, 8)),
        ],
        compiler_params=pltpu.CompilerParams(
            collective_id=0, has_side_effects=True, vmem_limit_bytes=40 << 20
        ),
    )(
        *(
            pltpu.with_memory_space_constraint(v, pltpu.HBM)
            for v in (
                concentration, geometry, nbr_elem, nbr_edge, wall_flags,
                jnp.asarray(forward), jnp.asarray(back), jnp.asarray(fourier), jnp.asarray(mass_b),
            )
        )
    )


def solution(mesh):
    return jax.shard_map(
        per_device,
        mesh=mesh,
        in_specs=(P("gz", None, "xy"), P(None, "xy"), P(None, "xy"), P(None, "xy"), P("gz")),
        out_specs=P("gz", None, "xy"),
        check_vma=False,
    )
```

```python
import functools

import jax
import jax.numpy as jnp
import ml_dtypes
import numpy as np
from jax import lax
from jax.experimental import pallas as pl
from jax.experimental.pallas import tpu as pltpu
from jax.sharding import PartitionSpec as P

time_step = 0.2
axial_stiffness = 0.002
edge_penalty = 4.0
axial_mobility = 0.002
mobility_floor = 0.05

MESH = pl.DeviceIdType.MESH
f32 = jnp.float32
bf16 = jnp.bfloat16


def point_tables():
    degree = 7
    points = np.arange(degree + 1)
    theta = np.pi * points / degree
    nodes_x = np.cos(theta)
    signs = np.where((points == 0) | (points == degree), 2.0, 1.0) * (-1.0) ** points
    differ = nodes_x[:, None] - nodes_x[None, :]
    deriv = np.outer(signs, 1.0 / signs) / (differ + np.eye(degree + 1))
    deriv = deriv - np.eye(degree + 1) * deriv.sum(axis=1)[:, None]
    inner = np.ones(degree - 1)
    for number in range(1, (degree - 1) // 2 + 1):
        inner = inner - 2.0 * np.cos(2 * number * theta[1:degree]) / (4 * number * number - 1)
    weights = np.zeros(degree + 1)
    weights[1:degree] = 2.0 * inner / degree
    weights[0] = 1.0 / degree**2
    weights[degree] = 1.0 / degree**2
    return (deriv, weights)


def fourier_table(length):
    planes = np.arange(length)
    wave_no = (planes + 1) // 2
    phase = np.outer(wave_no, planes) % length * (2.0 * np.pi / length)
    table = np.where((planes % 2 == 1)[:, None], np.cos(phase), np.sin(phase)) * np.sqrt(
        2.0 / length
    )
    table[0] = 1.0 / np.sqrt(length)
    table[length - 1] = np.cos(phase[length - 1]) / np.sqrt(length)
    return table


def parts(matrix):
    high = matrix.astype(ml_dtypes.bfloat16)
    low = (matrix - high.astype(np.float64)).astype(ml_dtypes.bfloat16)
    return high, low


def four(matrix):
    high, low = parts(matrix)
    return np.concatenate([high, high, low, low], axis=1)


def constants():
    deriv, weights = point_tables()
    grad_x = np.kron(np.eye(8), deriv)
    grad_y = np.kron(deriv, np.eye(8))
    mass = np.kron(weights, weights)
    forward = four(np.concatenate([grad_x, grad_y], axis=0))
    back = np.concatenate([four(grad_x.T * mass), four(grad_y.T * mass)], axis=1)
    table = fourier_table(256)
    wave = (np.arange(256) + 1) // 2
    scaled = -axial_mobility * (wave * wave)[:, None] * table
    fh, fl = parts(table)
    gh, gl = parts(scaled)
    fourier = np.concatenate([fh, fh, fl, gh, gh, gl], axis=1)
    mass_b = np.broadcast_to(mass[:, None], (64, 128)).astype(np.float32)
    line = deriv.T @ (weights[:, None] * deriv)
    return forward, back, fourier, mass_b, weights, line


def split(value):
    high = value.astype(bf16)
    return high, (value - high.astype(f32)).astype(bf16)


def split4(value):
    high, low = split(value)
    return jnp.concatenate([high, low, high, low], axis=0)


def dot(a, b):
    return jnp.dot(a, b, preferred_element_type=f32)


def lane_groups(shape):
    return lax.broadcasted_iota(jnp.int32, shape, 1) // 32


def swap4(x0, x1, x2, x3):
    group = lane_groups(x0.shape)
    low, even = group < 2, group % 2 == 0
    a0 = jnp.where(low, x0, pltpu.roll(x2, 64, 1))
    a2 = jnp.where(low, pltpu.roll(x0, 64, 1), x2)
    a1 = jnp.where(low, x1, pltpu.roll(x3, 64, 1))
    a3 = jnp.where(low, pltpu.roll(x1, 64, 1), x3)
    return (
        jnp.where(even, a0, pltpu.roll(a1, 32, 1)),
        jnp.where(even, pltpu.roll(a0, 96, 1), a1),
        jnp.where(even, a2, pltpu.roll(a3, 32, 1)),
        jnp.where(even, pltpu.roll(a2, 96, 1), a3),
    )


def node_of(edge, t):
    return (t, 8 * t + 7, 56 + t, 8 * t)[edge]


def apply_line(line, us):
    even = [us[m] + us[7 - m] for m in range(4)]
    odd = [us[m] - us[7 - m] for m in range(4)]
    out = [None] * 8
    for i in range(4):
        e = o = None
        for m in range(4):
            ce = float(0.5 * (line[i, m] + line[i, 7 - m]))
            co = float(0.5 * (line[i, m] - line[i, 7 - m]))
            e = ce * even[m] if e is None else e + ce * even[m]
            o = co * odd[m] if o is None else o + co * odd[m]
        out[i], out[7 - i] = e + o, e - o
    return out


def kernel(
    weights, line,
    c_ref, geo_hbm, nel_hbm, ned_hbm, flag_hbm, fwd_hbm, back_hbm, four_hbm, mass_hbm,
    out_ref,
    geo_ref, nel_ref, ned_ref, flag_ref, fwd_ref, back_ref, four_ref, mass_ref,
    cbuf, send1, recv1, ze, zb, send2, recv2, r0, q1, q2, rt, qt,
    lane_tab, src_tab, rev_tab, wall_tab, cross_tab, flag_tab, coef_tab, mc_tab,
    hsend, hrecv, dsend, drecv,
    csem, isem, s1sem, r1sem, s2sem, r2sem, hs_sem, hr_sem, ds_sem, dr_sem,
):
    xy = lax.axis_index("xy")
    gz = lax.axis_index("gz")
    z, x = gz // 4, gz % 4
    PHASES = ((1, 1), (1, 0), (0, 1), (0, 0))

    def tile_of(phase):
        return 2 * ((z + phase[0]) % 2) + (x + phase[1]) % 2

    def device_at(tile, d):
        return 4 * (2 * (d // 2) + tile // 2) + 2 * (d % 2) + tile % 2

    def d_of(j):
        return 2 * ((z // 2 + j // 2) % 2) + (x // 2 + j) % 2

    def load_c(i):
        tile = tile_of(PHASES[i])
        return pltpu.make_async_copy(
            c_ref.at[:, :, pl.ds(pl.multiple_of(tile * 128, 128), 128)], cbuf.at[i], csem.at[i]
        )

    for i in range(4):
        load_c(i).start()

    barrier = pltpu.get_barrier_semaphore()
    for d in range(1, 16):
        pl.semaphore_signal(barrier, 1, device_id=(xy, (gz + d) % 16), device_id_type=MESH)
    for d in range(1, 8):
        pl.semaphore_signal(barrier, 1, device_id=((xy + d) % 8, gz), device_id_type=MESH)

    loads = [
        pltpu.make_async_copy(src, dst, isem.at[i])
        for i, (src, dst) in enumerate(
            (
                (geo_hbm, geo_ref), (nel_hbm, nel_ref), (ned_hbm, ned_ref), (flag_hbm, flag_ref),
                (fwd_hbm, fwd_ref), (back_hbm, back_ref), (mass_hbm, mass_ref), (four_hbm, four_ref),
            )
        )
    ]
    for load in loads:
        load.start()

    for i in range(4):
        load_c(i).wait()

        def pack(pq, carry, i=i):
            tile = tile_of(PHASES[i])
            ys = swap4(*[cbuf[i, 4 * pq + pr] for pr in range(4)])
            for d in range(4):
                send1[device_at(tile, d), pq] = ys[d]
            return carry

        lax.fori_loop(0, 4, pack, 0)
    recv1[gz] = send1[gz]

    for load in loads:
        load.wait()
    scale_x, scale_y = geo_ref[0:1, :], geo_ref[1:2, :]
    jac = 1.0 / (scale_x * scale_y)
    my_tile, my_d = tile_of((0, 0)), d_of(0)
    for i, row in enumerate((jac, jac * scale_x * scale_x, jac * scale_y * scale_y)):
        mine = jnp.zeros((8, 128), f32)
        for tile in range(4):
            part = jnp.broadcast_to(row[:, 128 * tile : 128 * tile + 128], (8, 128))
            coef_tab[i, tile] = part
            group = lane_groups((8, 128))
            for d in range(4):
                one = jnp.where(group == d, part, 0.0)
                one = one + pltpu.roll(one, 64, 1)
                one = one + pltpu.roll(one, 32, 1)
                mine = jnp.where((my_tile == tile) & (my_d == d), one, mine)
        coef_tab[i, 4] = mine
    for a in range(4):
        for tile in range(4):
            cols = slice(128 * tile, 128 * tile + 128)
            elem = jnp.broadcast_to(nel_ref[a : a + 1, cols], (8, 128))
            code = jnp.broadcast_to(ned_ref[a : a + 1, cols], (8, 128))
            wall = elem < 0
            safe = jnp.maximum(elem, 0)
            owner = lax.shift_right_logical(safe, 9)
            local = safe & 511
            lane_tab[a, tile] = local & 127
            src_tab[a, tile] = jnp.where(
                wall, -1, jnp.where(owner == xy, (code & 3) * 4 + lax.shift_right_logical(local, 7), 16)
            )
            rev_tab[a, tile] = jnp.where(code >= 4, 1, 0)
            wall_tab[a, tile] = jnp.where(wall, 1, 0)
            cross_tab[a, tile] = jnp.where((owner != xy) & (elem >= 0), 1, 0)
    sub = lax.broadcasted_iota(jnp.int32, (8, 128), 0)
    for kh in range(2):
        flags = jnp.zeros((8, 128), f32)
        for k in range(8):
            flags = jnp.where(sub == k, flag_ref[8 * kh + k].astype(f32), flags)
        flag_tab[kh] = flags
        wave = lax.shift_right_logical(sub + 8 * kh + 16 * gz + 1, 1).astype(f32)
        mc_tab[kh] = 1.0 / time_step + axial_stiffness * wave * wave

    def source(s):
        a, b = 1 - s // 8, 1 - (s // 4) % 2
        return device_at(2 * ((z + a) % 2) + (x + b) % 2, d_of(s % 4))

    pl.semaphore_wait(barrier, 22)

    def copy1(h, pq):
        return pltpu.make_async_remote_copy(
            send1.at[h, pq], recv1.at[gz, pq], s1sem.at[h], r1sem.at[gz],
            device_id=(xy, h), device_id_type=MESH,
        )

    def block1(g):
        return pltpu.make_async_remote_copy(
            send1.at[g], recv1.at[g], s1sem.at[g], r1sem.at[g],
            device_id=(xy, g), device_id_type=MESH,
        )

    def others(i, act):
        def one(j, carry):
            h = source(4 * i + j)

            @pl.when(h != gz)
            def _():
                act(h)

            return carry

        lax.fori_loop(0, 4, one, 0)

    def issue1(i):
        for pq in range(4):
            others(i, lambda h, pq=pq: copy1(h, pq).start())

    for i in range(4):
        issue1(i)

    cj, ca, cb = (coef_tab[i, 4][0:1, :] for i in range(3))
    cj4, ca4, cb4 = (jnp.concatenate([v] * 4, axis=1) for v in (cj, ca, cb))
    mass4 = jnp.concatenate([mass_ref[...]] * 4, axis=1)

    def plane_terms(g):
        field = jnp.concatenate([recv1[g, pq] for pq in range(4)], axis=1)
        square = field * field
        chem = square * field - field
        mobility = jnp.maximum(1.0 - square, mobility_floor)
        along = dot(fwd_ref[...], split4(chem))
        flux_x = mobility * along[:64] * ca4
        flux_y = mobility * along[64:] * cb4
        both = jnp.concatenate([split4(flux_x), split4(flux_y)], axis=0)
        weak = dot(back_ref[...], both)
        weight = cj4 * mass4
        explicit = weight * field * (1.0 / time_step) - weak
        bulk = weight * chem
        for value, ref in ((explicit, ze), (bulk, zb)):
            for pq in range(4):
                cols = slice(128 * pq, 128 * pq + 128)
                for jh in range(2):
                    rows = [
                        value[8 * (4 * jh + jl) : 8 * (4 * jh + jl) + 8, cols] for jl in range(4)
                    ]
                    for pr, y in enumerate(swap4(*rows)):
                        start = (g * 16 + 4 * pq + pr) * 16 + 8 * jh
                        ref[pl.ds(pl.multiple_of(start, 8), 8), :] = y

    plane_terms(gz)

    def phase1(i, carry):
        def take(g):
            block1(g).wait_recv()
            plane_terms(g)

        others(i, take)
        return carry

    lax.fori_loop(0, 4, phase1, 0)

    def copy2(h, kh, which, start, size):
        rows = pl.ds(start, size)
        return pltpu.make_async_remote_copy(
            send2.at[h, kh, rows], recv2.at[gz, kh, rows], s2sem.at[h, which], r2sem.at[gz, kh],
            device_id=(xy, h), device_id_type=MESH,
        )

    def transform(rc, carry):
        blocks = []
        for ref in (ze, zb):
            pair = [ref[pl.ds(2 * rc + q, 256, stride=16), :] for q in range(2)]
            high, low = split(jnp.concatenate(pair, axis=1))
            blocks += [high, low, high]
        res = dot(four_ref[...], jnp.concatenate(blocks, axis=0))
        for h in range(16):
            for kh in range(2):
                for q in range(2):
                    row = 16 * h + 8 * kh
                    send2[h, kh, 2 * rc + q] = res[row : row + 8, 128 * q : 128 * q + 128]
        which = rc // 6
        for i in range(4):
            for j in range(4):
                if PHASES[i] == (0, 0) and j == 0:
                    continue
                copy2(device_at(tile_of(PHASES[i]), d_of(j)), 0, which, 2 * rc, 2).start()
        return carry

    lax.fori_loop(0, 8, transform, 0)
    recv2[gz] = send2[gz]


    def portion(p, act):
        others(p // 4, lambda h: act(copy2(h, 1, 2 + p % 4, 4 * (p % 4), 4)))

    def early(i, carry):
        others(i, lambda h: copy2(h, 0, 0, 0, 12).wait_send())
        return carry

    lax.fori_loop(0, 4, early, 0)
    for p in range(8):
        portion(p, lambda copy: copy.start())

    def arrived(kh, i):
        others(
            i,
            lambda g: pltpu.make_async_remote_copy(
                send2.at[g, kh], recv2.at[g, kh], s2sem.at[g, kh], r2sem.at[g, kh],
                device_id=(xy, g), device_id_type=MESH,
            ).wait_recv(),
        )

    def assemble(kh, tile):
        devices = [device_at(tile, d) for d in range(4)]
        for r in range(16):
            xs = [recv2[g, kh, r] for g in devices]
            for jl, y in enumerate(swap4(*xs)):
                r0[kh, tile, 32 * (r // 8) + 8 * jl + r % 8] = y

    def interior(src, dst, kh, tile):
        cj_t, ca_t, cb_t = (coef_tab[i, tile] for i in range(3))
        cjm = cj_t * mc_tab[kh]
        for j in range(8):
            us = [src[kh, tile, 8 * j + i] for i in range(8)]
            cjw, caw = cjm * float(weights[j]), ca_t * float(weights[j])
            for i, value in enumerate(apply_line(line, us)):
                dst[kh, tile, 8 * j + i] = caw * value + (cjw * float(weights[i])) * us[i]
        for i in range(8):
            us = [src[kh, tile, 8 * j + i] for j in range(8)]
            cbw = cb_t * float(weights[i])
            for j, value in enumerate(apply_line(line, us)):
                dst[kh, tile, 8 * j + i] = dst[kh, tile, 8 * j + i] + cbw * value

    def phase_tile(i):
        return 2 * ((z + 1 - i // 2) % 2) + (x + 1 - i % 2) % 2

    def gather_in(kh, i):
        arrived(kh, i)
        assemble(kh, phase_tile(i))

    def loop(n, body):
        def one(i, carry):
            body(i)
            return carry

        lax.fori_loop(0, n, one, 0)

    def second_pass(kh):
        def one(tile, carry):
            interior(q1, q2, kh, tile)
            return carry

        lax.fori_loop(0, 4, one, 0)

    def halo_copy(which, side):
        peer = (xy + (7, 1)[side]) % 8
        return pltpu.make_async_remote_copy(
            hsend.at[which, side], hrecv.at[which, side],
            hs_sem.at[which, side], hr_sem.at[which, side],
            device_id=(peer, gz), device_id_type=MESH,
        )

    def send_halo(ref, kh, which):
        for side, tile in ((0, 0), (1, 3)):
            on = [cross_tab[a, tile] > 0 for a in range(4)]
            for t in range(8):
                value = jnp.zeros((8, 128), f32)
                for a in range(4):
                    value = jnp.where(on[a], ref[kh, tile, node_of(a, t)], value)
                hsend[which, side, t] = value
            halo_copy(which, side).start()

    def pick(value, lane):
        return jnp.take_along_axis(value, lane, axis=1, mode="promise_in_bounds")

    def penalize(src, dst, kh):
        def one(tile, carry):
            flag = flag_tab[kh]
            for a in range(4):
                lane, src_id = lane_tab[a, tile], src_tab[a, tile]
                rev, wall = rev_tab[a, tile] > 0, wall_tab[a, tile] > 0
                factor = jnp.where(wall, flag, 1.0)
                for tp in range(4):
                    ts = (tp, 7 - tp)
                    weight = edge_penalty * float(weights[tp])
                    got = [jnp.zeros((8, 128), f32) for _ in ts]
                    for b in range(4):
                        for tile_b in range(4):
                            here = src_id == 4 * b + tile_b
                            for i, t in enumerate(ts):
                                picked = pick(src[kh, tile_b, node_of(b, t)], lane)
                                got[i] = jnp.where(here, picked, got[i])
                    for i, t in enumerate(ts):
                        at = node_of(a, t)
                        other = jnp.where(rev, got[1 - i], got[i])
                        pen = weight * (factor * src[kh, tile, at] - other)
                        dst[kh, tile, at] = dst[kh, tile, at] + pen
            return carry

        lax.fori_loop(0, 4, one, 0)

    def penalize_halo(dst, kh, which):
        for side in range(2):
            halo_copy(which, side).wait_recv()

        for tile, side in ((0, 1), (3, 0)):
            for a in range(4):
                lane, here = lane_tab[a, tile], src_tab[a, tile] == 16
                rev = rev_tab[a, tile] > 0
                for tp in range(4):
                    ts = (tp, 7 - tp)
                    weight = edge_penalty * float(weights[tp])
                    got = [pick(hrecv[which, side, t], lane) for t in ts]
                    for i, t in enumerate(ts):
                        at = node_of(a, t)
                        other = jnp.where(rev, got[1 - i], got[i])
                        dst[kh, tile, at] = dst[kh, tile, at] - jnp.where(here, weight * other, 0.0)

    def part_copy(which, g):
        return pltpu.make_async_remote_copy(
            dsend.at[which], drecv.at[which, xy], ds_sem.at[which, g], dr_sem.at[which, xy],
            device_id=(g, gz), device_id_type=MESH,
        )

    def total(which):
        for d in range(1, 8):
            part_copy(which, (xy + d) % 8).start()
        drecv[which, xy] = dsend[which]

    def total_done(which, n):
        for d in range(1, 8):
            g = (xy + d) % 8
            pltpu.make_async_remote_copy(
                dsend.at[which], drecv.at[which, g], ds_sem.at[which, g],
                dr_sem.at[which, g], device_id=(g, gz), device_id_type=MESH,
            ).wait_recv()
        out = []
        for i in range(n):
            acc = drecv[which, 0, i]
            for g in range(1, 8):
                acc = acc + drecv[which, g, i]
            out.append(jnp.broadcast_to(jnp.sum(acc, axis=1, keepdims=True), (8, 128)))
        return out

    def dots(which, n, terms):
        def one(tile, accs):
            accs = list(accs)
            for i in range(64):
                for m, term in enumerate(terms(tile, i)):
                    accs[2 * m + i % 2] = accs[2 * m + i % 2] + term
            return tuple(accs)

        accs = lax.fori_loop(0, 4, one, tuple(jnp.zeros((8, 128), f32) for _ in range(2 * n)))
        for m in range(n):
            dsend[which, m] = accs[2 * m] + accs[2 * m + 1]
        total(which)

    def first_matvec(kh):
        penalize(r0, q1, kh)
        penalize_halo(q1, kh, 2 * kh)
        send_halo(q1, kh, 2 * kh + 1)

        def terms1(tile, n):
            u, v = r0[kh, tile, n], q1[kh, tile, n]
            return u * u, u * v

        dots(2 * kh, 2, terms1)
        second_pass(kh)
        penalize(q1, q2, kh)

    def second_sums(kh):
        penalize_halo(q2, kh, 2 * kh + 1)
        rr0, pq0 = total_done(2 * kh, 2)
        alpha0 = rr0 / pq0

        def terms2(tile, n):
            u, v = r0[kh, tile, n], q1[kh, tile, n]
            r1 = u - alpha0 * v
            s = v - alpha0 * q2[kh, tile, n]
            return r1 * r1, r1 * s, r1 * v + u * s

        dots(2 * kh + 1, 3, terms2)
        return rr0, pq0

    def conclude(kh, rr0, pq0):
        def turn(tile, carry):
            for ref, out in ((r0, rt), (q1, qt)):
                rows = ref.reshape(2 * 4 * 64 * 8, 128)
                for j in range(8):
                    for k in range(8):
                        start = ((kh * 4 + tile) * 64 + 8 * j) * 8 + k
                        out[tile, k, 8 * j : 8 * j + 8, :] = rows[pl.ds(start, 8, stride=8), :]
            return carry

        lax.fori_loop(0, 4, turn, 0)
        rr1, r1s, cross = total_done(2 * kh + 1, 3)
        alpha0 = rr0 / pq0
        beta = rr1 / rr0
        alpha1 = rr1 / (r1s + beta * cross + beta * beta * pq0)
        along_r = alpha0 + alpha1 * (1.0 + beta)
        along_q = alpha1 * alpha0

        for tile in range(4):
            for k in range(8):
                out_ref[8 * kh + k, :, 128 * tile : 128 * tile + 128] = (
                    along_r[k : k + 1] * rt[tile, k] - along_q[k : k + 1] * qt[tile, k]
                )

    loop(4, lambda i: gather_in(0, i))
    send_halo(r0, 0, 0)
    for p in range(8, 16):
        portion(p, lambda copy: copy.start())
    loop(4, lambda tile: interior(r0, q1, 0, tile))
    first_matvec(0)

    def three(i):
        gather_in(1, i)
        interior(r0, q1, 1, phase_tile(i))

    loop(3, three)
    first_half = second_sums(0)
    gather_in(1, 3)
    send_halo(r0, 1, 2)
    interior(r0, q1, 1, phase_tile(3))
    first_matvec(1)
    second_half = second_sums(1)
    conclude(0, *first_half)
    conclude(1, *second_half)

    def sent(i, carry):
        others(i, lambda h: block1(h).wait_send())
        others(i, lambda h: copy2(h, 0, 1, 12, 4).wait_send())
        return carry

    lax.fori_loop(0, 4, sent, 0)
    for p in range(16):
        portion(p, lambda copy: copy.wait_send())
    for which in range(4):
        for side in range(2):
            halo_copy(which, side).wait_send()
        for d in range(1, 8):
            part_copy(which, (xy + d) % 8).wait_send()


def per_device(concentration, geometry, nbr_elem, nbr_edge, wall_flags):
    forward, back, fourier, mass_b, weights, line = constants()
    dma = pltpu.SemaphoreType.DMA
    V = pltpu.VMEM
    i32 = jnp.int32
    anywhere = pl.BlockSpec(memory_space=pl.ANY)
    return pl.pallas_call(
        functools.partial(kernel, weights, line),
        out_shape=jax.ShapeDtypeStruct(concentration.shape, f32),
        in_specs=[anywhere] * 9,
        out_specs=pl.BlockSpec(memory_space=pltpu.VMEM),
        scratch_shapes=[
            V((2, 512), f32),
            V((4, 512), i32),
            V((4, 512), i32),
            pltpu.SMEM((16,), i32),
            V(forward.shape, bf16),
            V(back.shape, bf16),
            V(fourier.shape, bf16),
            V((64, 128), f32),
            V((4, 16, 64, 128), f32),
            V((16, 4, 64, 128), f32),
            V((16, 4, 64, 128), f32),
            V((4096, 128), f32),
            V((4096, 128), f32),
            V((16, 2, 16, 8, 128), f32),
            V((16, 2, 16, 8, 128), f32),
            V((2, 4, 64, 8, 128), f32),
            V((2, 4, 64, 8, 128), f32),
            V((2, 4, 64, 8, 128), f32),
            V((4, 8, 64, 128), f32),
            V((4, 8, 64, 128), f32),
            V((4, 4, 8, 128), i32),
            V((4, 4, 8, 128), i32),
            V((4, 4, 8, 128), i32),
            V((4, 4, 8, 128), i32),
            V((4, 4, 8, 128), i32),
            V((2, 8, 128), f32),
            V((3, 5, 8, 128), f32),
            V((2, 8, 128), f32),
            V((4, 2, 8, 8, 128), f32),
            V((4, 2, 8, 8, 128), f32),
            V((4, 3, 8, 128), f32),
            V((4, 8, 3, 8, 128), f32),
            dma((4,)),
            dma((8,)),
            dma((16,)),
            dma((16,)),
            dma((16, 6)),
            dma((16, 2)),
            dma((4, 2)),
            dma((4, 2)),
            dma((4, 8)),
            dma((4, 8)),
        ],
        compiler_params=pltpu.CompilerParams(
            collective_id=0, has_side_effects=True, vmem_limit_bytes=40 << 20
        ),
    )(
        *(
            pltpu.with_memory_space_constraint(v, pltpu.HBM)
            for v in (
                concentration, geometry, nbr_elem, nbr_edge, wall_flags,
                jnp.asarray(forward), jnp.asarray(back), jnp.asarray(fourier), jnp.asarray(mass_b),
            )
        )
    )


def solution(mesh):
    return jax.shard_map(
        per_device,
        mesh=mesh,
        in_specs=(P("gz", None, "xy"), P(None, "xy"), P(None, "xy"), P(None, "xy"), P("gz")),
        out_specs=P("gz", None, "xy"),
        check_vma=False,
    )
```

```python
import functools

import jax
import jax.numpy as jnp
import ml_dtypes
import numpy as np
from jax import lax
from jax.experimental import pallas as pl
from jax.experimental.pallas import tpu as pltpu
from jax.sharding import PartitionSpec as P

time_step = 0.2
axial_stiffness = 0.002
edge_penalty = 4.0
axial_mobility = 0.002
mobility_floor = 0.05

MESH = pl.DeviceIdType.MESH
f32 = jnp.float32
bf16 = jnp.bfloat16


def point_tables():
    degree = 7
    points = np.arange(degree + 1)
    theta = np.pi * points / degree
    nodes_x = np.cos(theta)
    signs = np.where((points == 0) | (points == degree), 2.0, 1.0) * (-1.0) ** points
    differ = nodes_x[:, None] - nodes_x[None, :]
    deriv = np.outer(signs, 1.0 / signs) / (differ + np.eye(degree + 1))
    deriv = deriv - np.eye(degree + 1) * deriv.sum(axis=1)[:, None]
    inner = np.ones(degree - 1)
    for number in range(1, (degree - 1) // 2 + 1):
        inner = inner - 2.0 * np.cos(2 * number * theta[1:degree]) / (4 * number * number - 1)
    weights = np.zeros(degree + 1)
    weights[1:degree] = 2.0 * inner / degree
    weights[0] = 1.0 / degree**2
    weights[degree] = 1.0 / degree**2
    return (deriv, weights)


def fourier_table(length):
    planes = np.arange(length)
    wave_no = (planes + 1) // 2
    phase = np.outer(wave_no, planes) % length * (2.0 * np.pi / length)
    table = np.where((planes % 2 == 1)[:, None], np.cos(phase), np.sin(phase)) * np.sqrt(
        2.0 / length
    )
    table[0] = 1.0 / np.sqrt(length)
    table[length - 1] = np.cos(phase[length - 1]) / np.sqrt(length)
    return table


def parts(matrix):
    high = matrix.astype(ml_dtypes.bfloat16)
    low = (matrix - high.astype(np.float64)).astype(ml_dtypes.bfloat16)
    return high, low


def four(matrix):
    high, low = parts(matrix)
    return np.concatenate([high, high, low, low], axis=1)


def constants():
    deriv, weights = point_tables()
    grad_x = np.kron(np.eye(8), deriv)
    grad_y = np.kron(deriv, np.eye(8))
    mass = np.kron(weights, weights)
    forward = four(np.concatenate([grad_x, grad_y], axis=0))
    back = np.concatenate([four(grad_x.T * mass), four(grad_y.T * mass)], axis=1)
    table = fourier_table(256)
    wave = (np.arange(256) + 1) // 2
    scaled = -axial_mobility * (wave * wave)[:, None] * table
    fh, fl = parts(table)
    gh, gl = parts(scaled)
    fourier = np.concatenate([fh, fh, fl, gh, gh, gl], axis=1)
    mass_b = np.broadcast_to(mass[:, None], (64, 128)).astype(np.float32)
    line = deriv.T @ (weights[:, None] * deriv)
    return forward, back, fourier, mass_b, weights, line


def split(value):
    high = value.astype(bf16)
    return high, (value - high.astype(f32)).astype(bf16)


def split4(value):
    high, low = split(value)
    return jnp.concatenate([high, low, high, low], axis=0)


def dot(a, b):
    return jnp.dot(a, b, preferred_element_type=f32)


def lane_groups(shape):
    return lax.broadcasted_iota(jnp.int32, shape, 1) // 32


def swap4(x0, x1, x2, x3):
    group = lane_groups(x0.shape)
    low, even = group < 2, group % 2 == 0
    a0 = jnp.where(low, x0, pltpu.roll(x2, 64, 1))
    a2 = jnp.where(low, pltpu.roll(x0, 64, 1), x2)
    a1 = jnp.where(low, x1, pltpu.roll(x3, 64, 1))
    a3 = jnp.where(low, pltpu.roll(x1, 64, 1), x3)
    return (
        jnp.where(even, a0, pltpu.roll(a1, 32, 1)),
        jnp.where(even, pltpu.roll(a0, 96, 1), a1),
        jnp.where(even, a2, pltpu.roll(a3, 32, 1)),
        jnp.where(even, pltpu.roll(a2, 96, 1), a3),
    )


def node_of(edge, t):
    return (t, 8 * t + 7, 56 + t, 8 * t)[edge]


def apply_line(line, us):
    even = [us[m] + us[7 - m] for m in range(4)]
    odd = [us[m] - us[7 - m] for m in range(4)]
    out = [None] * 8
    for i in range(4):
        e = o = None
        for m in range(4):
            ce = float(0.5 * (line[i, m] + line[i, 7 - m]))
            co = float(0.5 * (line[i, m] - line[i, 7 - m]))
            e = ce * even[m] if e is None else e + ce * even[m]
            o = co * odd[m] if o is None else o + co * odd[m]
        out[i], out[7 - i] = e + o, e - o
    return out


def kernel(
    weights, line,
    c_ref, geo_hbm, nel_hbm, ned_hbm, flag_hbm, fwd_hbm, back_hbm, four_hbm, mass_hbm,
    out_ref,
    geo_ref, nel_ref, ned_ref, flag_ref, fwd_ref, back_ref, four_ref, mass_ref,
    cbuf, send1, recv1, ze, zb, send2, recv2, r0, q1, q2, rt, qt,
    lane_tab, src_tab, rev_tab, wall_tab, cross_tab, flag_tab, coef_tab, mc_tab,
    hsend, hrecv, dsend, drecv,
    csem, isem, s1sem, r1sem, s2sem, r2sem, hs_sem, hr_sem, ds_sem, dr_sem,
):
    xy = lax.axis_index("xy")
    gz = lax.axis_index("gz")
    z, x = gz // 4, gz % 4
    PHASES = ((1, 1), (1, 0), (0, 1), (0, 0))

    def tile_of(phase):
        return 2 * ((z + phase[0]) % 2) + (x + phase[1]) % 2

    def device_at(tile, d):
        return 4 * (2 * (d // 2) + tile // 2) + 2 * (d % 2) + tile % 2

    def d_of(j):
        return 2 * ((z // 2 + j // 2) % 2) + (x // 2 + j) % 2

    def load_c(i):
        tile = tile_of(PHASES[i])
        return pltpu.make_async_copy(
            c_ref.at[:, :, pl.ds(pl.multiple_of(tile * 128, 128), 128)], cbuf.at[i], csem.at[i]
        )

    for i in range(4):
        load_c(i).start()

    barrier = pltpu.get_barrier_semaphore()
    for d in range(1, 16):
        pl.semaphore_signal(barrier, 1, device_id=(xy, (gz + d) % 16), device_id_type=MESH)
    for d in range(1, 8):
        pl.semaphore_signal(barrier, 1, device_id=((xy + d) % 8, gz), device_id_type=MESH)

    loads = [
        pltpu.make_async_copy(src, dst, isem.at[i])
        for i, (src, dst) in enumerate(
            (
                (geo_hbm, geo_ref), (nel_hbm, nel_ref), (ned_hbm, ned_ref), (flag_hbm, flag_ref),
                (fwd_hbm, fwd_ref), (back_hbm, back_ref), (mass_hbm, mass_ref), (four_hbm, four_ref),
            )
        )
    ]
    for load in loads:
        load.start()

    for i in range(4):
        load_c(i).wait()

        def pack(pq, carry, i=i):
            tile = tile_of(PHASES[i])
            ys = swap4(*[cbuf[i, 4 * pq + pr] for pr in range(4)])
            for d in range(4):
                send1[device_at(tile, d), pq] = ys[d]
            return carry

        lax.fori_loop(0, 4, pack, 0)
    recv1[gz] = send1[gz]

    for load in loads:
        load.wait()
    scale_x, scale_y = geo_ref[0:1, :], geo_ref[1:2, :]
    jac = 1.0 / (scale_x * scale_y)
    my_tile, my_d = tile_of((0, 0)), d_of(0)
    for i, row in enumerate((jac, jac * scale_x * scale_x, jac * scale_y * scale_y)):
        mine = jnp.zeros((8, 128), f32)
        for tile in range(4):
            part = jnp.broadcast_to(row[:, 128 * tile : 128 * tile + 128], (8, 128))
            coef_tab[i, tile] = part
            group = lane_groups((8, 128))
            for d in range(4):
                one = jnp.where(group == d, part, 0.0)
                one = one + pltpu.roll(one, 64, 1)
                one = one + pltpu.roll(one, 32, 1)
                mine = jnp.where((my_tile == tile) & (my_d == d), one, mine)
        coef_tab[i, 4] = mine
    for a in range(4):
        for tile in range(4):
            cols = slice(128 * tile, 128 * tile + 128)
            elem = jnp.broadcast_to(nel_ref[a : a + 1, cols], (8, 128))
            code = jnp.broadcast_to(ned_ref[a : a + 1, cols], (8, 128))
            wall = elem < 0
            safe = jnp.maximum(elem, 0)
            owner = lax.shift_right_logical(safe, 9)
            local = safe & 511
            lane_tab[a, tile] = local & 127
            src_tab[a, tile] = jnp.where(
                wall, -1, jnp.where(owner == xy, (code & 3) * 4 + lax.shift_right_logical(local, 7), 16)
            )
            rev_tab[a, tile] = jnp.where(code >= 4, 1, 0)
            wall_tab[a, tile] = jnp.where(wall, 1, 0)
            cross_tab[a, tile] = jnp.where((owner != xy) & (elem >= 0), 1, 0)
    sub = lax.broadcasted_iota(jnp.int32, (8, 128), 0)
    for kh in range(2):
        flags = jnp.zeros((8, 128), f32)
        for k in range(8):
            flags = jnp.where(sub == k, flag_ref[8 * kh + k].astype(f32), flags)
        flag_tab[kh] = flags
        wave = lax.shift_right_logical(sub + 8 * kh + 16 * gz + 1, 1).astype(f32)
        mc_tab[kh] = 1.0 / time_step + axial_stiffness * wave * wave

    def source(s):
        a, b = 1 - s // 8, 1 - (s // 4) % 2
        return device_at(2 * ((z + a) % 2) + (x + b) % 2, d_of(s % 4))

    pl.semaphore_wait(barrier, 22)

    def copy1(h, pq):
        return pltpu.make_async_remote_copy(
            send1.at[h, pq], recv1.at[gz, pq], s1sem.at[h], r1sem.at[gz],
            device_id=(xy, h), device_id_type=MESH,
        )

    def block1(g):
        return pltpu.make_async_remote_copy(
            send1.at[g], recv1.at[g], s1sem.at[g], r1sem.at[g],
            device_id=(xy, g), device_id_type=MESH,
        )

    def others(i, act):
        def one(j, carry):
            h = source(4 * i + j)

            @pl.when(h != gz)
            def _():
                act(h)

            return carry

        lax.fori_loop(0, 4, one, 0)

    def issue1(i):
        for pq in range(4):
            others(i, lambda h, pq=pq: copy1(h, pq).start())

    for i in range(4):
        issue1(i)

    cj, ca, cb = (coef_tab[i, 4][0:1, :] for i in range(3))
    cj4, ca4, cb4 = (jnp.concatenate([v] * 4, axis=1) for v in (cj, ca, cb))
    mass4 = jnp.concatenate([mass_ref[...]] * 4, axis=1)

    def plane_terms(g):
        field = jnp.concatenate([recv1[g, pq] for pq in range(4)], axis=1)
        square = field * field
        chem = square * field - field
        mobility = jnp.maximum(1.0 - square, mobility_floor)
        along = dot(fwd_ref[...], split4(chem))
        flux_x = mobility * along[:64] * ca4
        flux_y = mobility * along[64:] * cb4
        both = jnp.concatenate([split4(flux_x), split4(flux_y)], axis=0)
        weak = dot(back_ref[...], both)
        weight = cj4 * mass4
        explicit = weight * field * (1.0 / time_step) - weak
        bulk = weight * chem
        for value, ref in ((explicit, ze), (bulk, zb)):
            for pq in range(4):
                cols = slice(128 * pq, 128 * pq + 128)
                for jh in range(2):
                    rows = [
                        value[8 * (4 * jh + jl) : 8 * (4 * jh + jl) + 8, cols] for jl in range(4)
                    ]
                    for pr, y in enumerate(swap4(*rows)):
                        start = (g * 16 + 4 * pq + pr) * 16 + 8 * jh
                        ref[pl.ds(pl.multiple_of(start, 8), 8), :] = y

    plane_terms(gz)

    def take(*places):
        for p in places:
            block1(source(p)).wait_recv()
        for p in places:
            plane_terms(source(p))

    def phase1(i, carry):
        take(2 * i, 2 * i + 1)
        return carry

    lax.fori_loop(0, 6, phase1, 0)
    take(13)
    take(14, 15)

    def copy2(h, kh, which, start, size):
        rows = pl.ds(start, size)
        return pltpu.make_async_remote_copy(
            send2.at[h, kh, rows], recv2.at[gz, kh, rows], s2sem.at[h, which], r2sem.at[gz, kh],
            device_id=(xy, h), device_id_type=MESH,
        )

    def transform(rc, carry):
        blocks = []
        for ref in (ze, zb):
            pair = [ref[pl.ds(2 * rc + q, 256, stride=16), :] for q in range(2)]
            high, low = split(jnp.concatenate(pair, axis=1))
            blocks += [high, low, high]
        res = dot(four_ref[...], jnp.concatenate(blocks, axis=0))
        for h in range(16):
            for kh in range(2):
                for q in range(2):
                    row = 16 * h + 8 * kh
                    send2[h, kh, 2 * rc + q] = res[row : row + 8, 128 * q : 128 * q + 128]
        which = rc // 6
        for i in range(4):
            for j in range(4):
                if PHASES[i] == (0, 0) and j == 0:
                    continue
                copy2(device_at(tile_of(PHASES[i]), d_of(j)), 0, which, 2 * rc, 2).start()
        return carry

    lax.fori_loop(0, 8, transform, 0)
    recv2[gz] = send2[gz]


    def portion(p, act):
        others(p // 4, lambda h: act(copy2(h, 1, 2 + p % 4, 4 * (p % 4), 4)))

    def early(i, carry):
        others(i, lambda h: copy2(h, 0, 0, 0, 12).wait_send())
        return carry

    lax.fori_loop(0, 4, early, 0)
    for p in range(8):
        portion(p, lambda copy: copy.start())

    def arrived(kh, i):
        others(
            i,
            lambda g: pltpu.make_async_remote_copy(
                send2.at[g, kh], recv2.at[g, kh], s2sem.at[g, kh], r2sem.at[g, kh],
                device_id=(xy, g), device_id_type=MESH,
            ).wait_recv(),
        )

    def assemble(kh, tile):
        devices = [device_at(tile, d) for d in range(4)]
        for r in range(16):
            xs = [recv2[g, kh, r] for g in devices]
            for jl, y in enumerate(swap4(*xs)):
                r0[kh, tile, 32 * (r // 8) + 8 * jl + r % 8] = y

    def interior(src, dst, kh, tile):
        cj_t, ca_t, cb_t = (coef_tab[i, tile] for i in range(3))
        cjm = cj_t * mc_tab[kh]
        for j in range(8):
            us = [src[kh, tile, 8 * j + i] for i in range(8)]
            cjw, caw = cjm * float(weights[j]), ca_t * float(weights[j])
            for i, value in enumerate(apply_line(line, us)):
                dst[kh, tile, 8 * j + i] = caw * value + (cjw * float(weights[i])) * us[i]
        for i in range(8):
            us = [src[kh, tile, 8 * j + i] for j in range(8)]
            cbw = cb_t * float(weights[i])
            for j, value in enumerate(apply_line(line, us)):
                dst[kh, tile, 8 * j + i] = dst[kh, tile, 8 * j + i] + cbw * value

    def phase_tile(i):
        return 2 * ((z + 1 - i // 2) % 2) + (x + 1 - i % 2) % 2

    def gather_in(kh, i):
        arrived(kh, i)
        assemble(kh, phase_tile(i))

    def loop(n, body):
        def one(i, carry):
            body(i)
            return carry

        lax.fori_loop(0, n, one, 0)

    def second_pass(kh):
        def one(tile, carry):
            interior(q1, q2, kh, tile)
            return carry

        lax.fori_loop(0, 4, one, 0)

    def halo_copy(which, side):
        peer = (xy + (7, 1)[side]) % 8
        return pltpu.make_async_remote_copy(
            hsend.at[which, side], hrecv.at[which, side],
            hs_sem.at[which, side], hr_sem.at[which, side],
            device_id=(peer, gz), device_id_type=MESH,
        )

    def send_halo(ref, kh, which):
        for side, tile in ((0, 0), (1, 3)):
            on = [cross_tab[a, tile] > 0 for a in range(4)]
            for t in range(8):
                value = jnp.zeros((8, 128), f32)
                for a in range(4):
                    value = jnp.where(on[a], ref[kh, tile, node_of(a, t)], value)
                hsend[which, side, t] = value
            halo_copy(which, side).start()

    def pick(value, lane):
        return jnp.take_along_axis(value, lane, axis=1, mode="promise_in_bounds")

    def penalize(src, dst, kh):
        def one(tile, carry):
            flag = flag_tab[kh]
            for a in range(4):
                lane, src_id = lane_tab[a, tile], src_tab[a, tile]
                rev, wall = rev_tab[a, tile] > 0, wall_tab[a, tile] > 0
                factor = jnp.where(wall, flag, 1.0)
                for tp in range(4):
                    ts = (tp, 7 - tp)
                    weight = edge_penalty * float(weights[tp])
                    got = [jnp.zeros((8, 128), f32) for _ in ts]
                    for b in range(4):
                        for tile_b in range(4):
                            here = src_id == 4 * b + tile_b
                            for i, t in enumerate(ts):
                                picked = pick(src[kh, tile_b, node_of(b, t)], lane)
                                got[i] = jnp.where(here, picked, got[i])
                    for i, t in enumerate(ts):
                        at = node_of(a, t)
                        other = jnp.where(rev, got[1 - i], got[i])
                        pen = weight * (factor * src[kh, tile, at] - other)
                        dst[kh, tile, at] = dst[kh, tile, at] + pen
            return carry

        lax.fori_loop(0, 4, one, 0)

    def penalize_halo(dst, kh, which):
        for side in range(2):
            halo_copy(which, side).wait_recv()

        for tile, side in ((0, 1), (3, 0)):
            for a in range(4):
                lane, here = lane_tab[a, tile], src_tab[a, tile] == 16
                rev = rev_tab[a, tile] > 0
                for tp in range(4):
                    ts = (tp, 7 - tp)
                    weight = edge_penalty * float(weights[tp])
                    got = [pick(hrecv[which, side, t], lane) for t in ts]
                    for i, t in enumerate(ts):
                        at = node_of(a, t)
                        other = jnp.where(rev, got[1 - i], got[i])
                        dst[kh, tile, at] = dst[kh, tile, at] - jnp.where(here, weight * other, 0.0)

    def part_copy(which, g):
        return pltpu.make_async_remote_copy(
            dsend.at[which], drecv.at[which, xy], ds_sem.at[which, g], dr_sem.at[which, xy],
            device_id=(g, gz), device_id_type=MESH,
        )

    def total(which):
        for d in range(1, 8):
            part_copy(which, (xy + d) % 8).start()
        drecv[which, xy] = dsend[which]

    def total_done(which, n):
        for d in range(1, 8):
            g = (xy + d) % 8
            pltpu.make_async_remote_copy(
                dsend.at[which], drecv.at[which, g], ds_sem.at[which, g],
                dr_sem.at[which, g], device_id=(g, gz), device_id_type=MESH,
            ).wait_recv()
        acc = drecv[which, 0]
        for g in range(1, 8):
            acc = acc + drecv[which, g]
        group = lane_groups((8, 128))
        out = []
        for m in range(n):
            mine = jnp.sum(jnp.where(group == m, acc, 0.0), axis=1, keepdims=True)
            out.append(jnp.broadcast_to(mine, (8, 128)))
        return out

    def dots(which, n, terms):
        def one(tile, accs):
            accs = list(accs)
            for i in range(64):
                for m, term in enumerate(terms(tile, i)):
                    accs[2 * m + i % 2] = accs[2 * m + i % 2] + term
            return tuple(accs)

        accs = lax.fori_loop(0, 4, one, tuple(jnp.zeros((8, 128), f32) for _ in range(2 * n)))
        group = lane_groups((8, 128))
        packed = jnp.zeros((8, 128), f32)
        for m in range(n):
            folded = accs[2 * m] + accs[2 * m + 1]
            folded = folded + pltpu.roll(folded, 64, 1)
            folded = folded + pltpu.roll(folded, 32, 1)
            packed = jnp.where(group == m, folded, packed)
        dsend[which] = packed
        total(which)

    def first_matvec(kh):
        penalize(r0, q1, kh)
        penalize_halo(q1, kh, 2 * kh)
        send_halo(q1, kh, 2 * kh + 1)

        def terms1(tile, n):
            u, v = r0[kh, tile, n], q1[kh, tile, n]
            return u * u, u * v

        dots(2 * kh, 2, terms1)
        second_pass(kh)
        penalize(q1, q2, kh)

    def second_sums(kh):
        penalize_halo(q2, kh, 2 * kh + 1)
        rr0, pq0 = total_done(2 * kh, 2)
        alpha0 = rr0 / pq0

        def terms2(tile, n):
            u, v = r0[kh, tile, n], q1[kh, tile, n]
            r1 = u - alpha0 * v
            s = v - alpha0 * q2[kh, tile, n]
            return r1 * r1, r1 * s, r1 * v + u * s

        dots(2 * kh + 1, 3, terms2)
        return rr0, pq0

    def conclude(kh, rr0, pq0):
        def turn(tile, carry):
            for ref, out in ((r0, rt), (q1, qt)):
                rows = ref.reshape(2 * 4 * 64 * 8, 128)
                for j in range(8):
                    for k in range(8):
                        start = ((kh * 4 + tile) * 64 + 8 * j) * 8 + k
                        out[tile, k, 8 * j : 8 * j + 8, :] = rows[pl.ds(start, 8, stride=8), :]
            return carry

        lax.fori_loop(0, 4, turn, 0)
        rr1, r1s, cross = total_done(2 * kh + 1, 3)
        alpha0 = rr0 / pq0
        beta = rr1 / rr0
        alpha1 = rr1 / (r1s + beta * cross + beta * beta * pq0)
        along_r = alpha0 + alpha1 * (1.0 + beta)
        along_q = alpha1 * alpha0

        for tile in range(4):
            for k in range(8):
                out_ref[8 * kh + k, :, 128 * tile : 128 * tile + 128] = (
                    along_r[k : k + 1] * rt[tile, k] - along_q[k : k + 1] * qt[tile, k]
                )

    loop(4, lambda i: gather_in(0, i))
    send_halo(r0, 0, 0)
    for p in range(8, 16):
        portion(p, lambda copy: copy.start())
    loop(4, lambda tile: interior(r0, q1, 0, tile))
    first_matvec(0)

    def three(i):
        gather_in(1, i)
        interior(r0, q1, 1, phase_tile(i))

    loop(3, three)
    first_half = second_sums(0)
    gather_in(1, 3)
    send_halo(r0, 1, 2)
    interior(r0, q1, 1, phase_tile(3))
    first_matvec(1)
    second_half = second_sums(1)
    conclude(0, *first_half)
    conclude(1, *second_half)

    def sent(i, carry):
        others(i, lambda h: block1(h).wait_send())
        others(i, lambda h: copy2(h, 0, 1, 12, 4).wait_send())
        return carry

    lax.fori_loop(0, 4, sent, 0)
    for p in range(16):
        portion(p, lambda copy: copy.wait_send())
    for which in range(4):
        for side in range(2):
            halo_copy(which, side).wait_send()
        for d in range(1, 8):
            part_copy(which, (xy + d) % 8).wait_send()


def per_device(concentration, geometry, nbr_elem, nbr_edge, wall_flags):
    forward, back, fourier, mass_b, weights, line = constants()
    dma = pltpu.SemaphoreType.DMA
    V = pltpu.VMEM
    i32 = jnp.int32
    anywhere = pl.BlockSpec(memory_space=pl.ANY)
    return pl.pallas_call(
        functools.partial(kernel, weights, line),
        out_shape=jax.ShapeDtypeStruct(concentration.shape, f32),
        in_specs=[anywhere] * 9,
        out_specs=pl.BlockSpec(memory_space=pltpu.VMEM),
        scratch_shapes=[
            V((2, 512), f32),
            V((4, 512), i32),
            V((4, 512), i32),
            pltpu.SMEM((16,), i32),
            V(forward.shape, bf16),
            V(back.shape, bf16),
            V(fourier.shape, bf16),
            V((64, 128), f32),
            V((4, 16, 64, 128), f32),
            V((16, 4, 64, 128), f32),
            V((16, 4, 64, 128), f32),
            V((4096, 128), f32),
            V((4096, 128), f32),
            V((16, 2, 16, 8, 128), f32),
            V((16, 2, 16, 8, 128), f32),
            V((2, 4, 64, 8, 128), f32),
            V((2, 4, 64, 8, 128), f32),
            V((2, 4, 64, 8, 128), f32),
            V((4, 8, 64, 128), f32),
            V((4, 8, 64, 128), f32),
            V((4, 4, 8, 128), i32),
            V((4, 4, 8, 128), i32),
            V((4, 4, 8, 128), i32),
            V((4, 4, 8, 128), i32),
            V((4, 4, 8, 128), i32),
            V((2, 8, 128), f32),
            V((3, 5, 8, 128), f32),
            V((2, 8, 128), f32),
            V((4, 2, 8, 8, 128), f32),
            V((4, 2, 8, 8, 128), f32),
            V((4, 8, 128), f32),
            V((4, 8, 8, 128), f32),
            dma((4,)),
            dma((8,)),
            dma((16,)),
            dma((16,)),
            dma((16, 6)),
            dma((16, 2)),
            dma((4, 2)),
            dma((4, 2)),
            dma((4, 8)),
            dma((4, 8)),
        ],
        compiler_params=pltpu.CompilerParams(
            collective_id=0, has_side_effects=True, vmem_limit_bytes=40 << 20
        ),
    )(
        *(
            pltpu.with_memory_space_constraint(v, pltpu.HBM)
            for v in (
                concentration, geometry, nbr_elem, nbr_edge, wall_flags,
                jnp.asarray(forward), jnp.asarray(back), jnp.asarray(fourier), jnp.asarray(mass_b),
            )
        )
    )


def solution(mesh):
    return jax.shard_map(
        per_device,
        mesh=mesh,
        in_specs=(P("gz", None, "xy"), P(None, "xy"), P(None, "xy"), P(None, "xy"), P("gz")),
        out_specs=P("gz", None, "xy"),
        check_vma=False,
    )
```
